128 devices in a mesh: grp: 2 (over z_lo), head: 64 (over y, z_hi, x, core).
Axes of the slice: x: 4, y: 4, z: 4 (z_hi: 2, z_lo: 2; z = z_hi * 2 + z_lo), core: 2. Of those that a mesh axis runs over, the one named last changes fastest.
Arguments:
- query: bfloat16 [72, 256, 8192], P('grp', 'head'), may hold values from -24 to 24
- out_grad: bfloat16 [72, 256, 8192], P('grp', 'head'), may hold values from -6 to 6
- forward_out: bfloat16 [72, 256, 8192], P('grp', 'head'), may hold values from -6 to 6
- key_codes: bfloat16 [4, 256, 8192], P('grp', 'head'), may hold values from -127 to 127, as said below
- key_scale: bfloat16 [4, 256, 64], P('grp', 'head'), may hold values from 0.0039 to 0.0402
- value_codes: bfloat16 [4, 256, 8192], P('grp', 'head'), may hold values from -127 to 127, as said below
- value_scale: bfloat16 [4, 256, 64], P('grp', 'head'), may hold values from 0.0039 to 0.0402
- pairing: int32 [72, 2], replicated, may hold values from 0 to 3, as said below
Outputs:
- grad_query: bfloat16 [72, 256, 8192], P('grp', 'head')
- grad_key: bfloat16 [4, 256, 8192], P('grp', 'head')
- grad_value: bfloat16 [4, 256, 8192], P('grp', 'head')
The draws below stay inside these ranges and needn't reach their ends.
Inputs may be any that keep to these rules, and one draw needn't show every extreme that they name: `key_codes`: whole numbers. `value_codes`: whole numbers. `pairing`: the two entries of a row differ.
All inputs are finite; a program needn't handle non-finite values.
Results may differ from the reference program's by a relative error of at most 0.012.
The reference program's roundings to bfloat16 on the way (of `keys`, `values`, `key_set`, `rounded` and `score_grad`) count: a program that leaves them out, or rounds other values in their place, can miss the bound.
Values may be sent and summed in bfloat16 or wider, within the bound.
No kernel may reach another device: no remote copies, remote signals or barrier semaphores. Data moves between devices by JAX's collectives and lax.ppermute only.
A program may use at most 192 MiB of HBM per device.

```python
import math
import jax
import jax.numpy as jnp
from jax import lax

HD = 128
H = 64
D = 8192
L = 256
QC = 72
KC = 4


def kv_tables(key):
    low = math.log(0.004)
    high = math.log(0.04)
    key_part = jax.random.randint(jax.random.fold_in(key, 101), (KC, L, D), -127, 128).astype(jnp.float32)
    key_scales = jnp.exp(jax.random.uniform(jax.random.fold_in(key, 102), (KC, L, H), minval=low, maxval=high))
    value_part = jax.random.randint(jax.random.fold_in(key, 103), (KC, L, D), -127, 128).astype(jnp.float32)
    value_scales = jnp.exp(jax.random.uniform(jax.random.fold_in(key, 104), (KC, L, H), minval=low, maxval=high))
    return (key_part, key_scales, value_part, value_scales)


def pair_table(key):
    row_keys = jax.random.split(jax.random.fold_in(key, 301), QC)
    return jax.vmap(lambda row_key: jax.random.permutation(row_key, KC)[:2])(row_keys).astype(jnp.int32)


def draw_query(key, part):
    result = jnp.clip(jax.random.normal(jax.random.fold_in(key, 201), (QC, L, D)), -6.0, 6.0)
    return result.astype(jnp.bfloat16)


def draw_key_codes(key, part):
    return kv_tables(key)[0].astype(jnp.bfloat16)


def draw_key_scale(key, part):
    return kv_tables(key)[1].astype(jnp.bfloat16)


def draw_value_codes(key, part):
    return kv_tables(key)[2].astype(jnp.bfloat16)


def draw_value_scale(key, part):
    return kv_tables(key)[3].astype(jnp.bfloat16)


def draw_pairing(key, part):
    return pair_table(key)


def levels(own_key, dims, shards, least, high):
    level, own = 1.0, jax.random.fold_in(own_key, 6)
    for axis_at, shards_of in shards:
        heights = jnp.exp(jax.random.uniform(jax.random.fold_in(own, axis_at), (shards_of,), jnp.float32, least / len(shards), high / len(shards)))
        level = level * jnp.repeat(heights, dims[axis_at] // shards_of).reshape([-1 if axis == axis_at else 1 for axis in range(len(dims))])
    return level


def normal_values(stream_key, extent, spread, reach, cuts=(), held_as=jnp.bfloat16):
    gain = levels(stream_key, extent, cuts, -0.22, 0.18) if cuts else 1.0
    drawn = jax.random.normal(stream_key, extent, jnp.float32) * spread * gain
    return jnp.minimum(jnp.maximum(drawn, -reach), reach).astype(held_as)


def setup_inputs(seed: int = 0) -> dict:
    keys = jax.random.split(jax.random.key(seed), 9)
    return {
        "query": draw_query(jax.random.fold_in(keys[8], 71), 0),
        "out_grad": normal_values(keys[1], (QC, L, D), 1.0, 6.0, ((0, 2), (1, 64))),
        "forward_out": normal_values(keys[2], (QC, L, D), 1.0, 6.0, ((0, 2), (1, 64))),
        "key_codes": draw_key_codes(jax.random.fold_in(keys[8], 71), 0),
        "key_scale": draw_key_scale(jax.random.fold_in(keys[8], 71), 0),
        "value_codes": draw_value_codes(jax.random.fold_in(keys[8], 71), 0),
        "value_scale": draw_value_scale(jax.random.fold_in(keys[8], 71), 0),
        "pairing": draw_pairing(jax.random.fold_in(keys[8], 71), 0),
    }


def dequantize(codes, scales):
    count, length, width = codes.shape
    head_count = scales.shape[2]
    values = codes.astype(jnp.float32).reshape(count, length, head_count, width // head_count) * scales.astype(jnp.float32)[..., None]
    return values.reshape(count, length, width).astype(jnp.bfloat16)


def per_head(array):
    return array.reshape(array.shape[0], L, H, HD).transpose(2, 0, 1, 3)


def to_rows(array):
    return array.transpose(1, 2, 0, 3).reshape(array.shape[1], L, D)


def reference(query, out_grad, forward_out, key_codes, key_scale, value_codes, value_scale, pairing):
    softmax_scale = HD ** -0.5
    key_full = dequantize(key_codes, key_scale)
    value_full = dequantize(value_codes, value_scale)
    product = out_grad.astype(jnp.float32) * forward_out.astype(jnp.float32)
    row_dots = jnp.sum(product.reshape(QC, L, H, HD), axis=-1).transpose(2, 0, 1)

    def one_head(inputs):
        query_head, grad_head, dot_head, key_head, value_head = inputs
        key_acc = jnp.zeros((KC, L, HD), jnp.float32)
        value_acc = jnp.zeros((KC, L, HD), jnp.float32)
        query_out = []
        for block_pos in range(QC):
            chosen = pairing[block_pos]
            key_set = jnp.take(key_head, chosen, axis=0).reshape(2 * L, HD)
            value_set = jnp.take(value_head, chosen, axis=0).reshape(2 * L, HD)
            scores = jnp.dot(query_head[block_pos], key_set.T, preferred_element_type=jnp.float32) * softmax_scale
            highest = jnp.max(scores, axis=1)
            weights = jnp.exp(scores - highest[:, None])
            probs = weights / jnp.sum(weights, axis=1)[:, None]
            rounded = probs.astype(jnp.bfloat16)
            value_grad = jnp.dot(rounded.T, grad_head[block_pos], preferred_element_type=jnp.float32)
            prob_grad = jnp.dot(grad_head[block_pos], value_set.T, preferred_element_type=jnp.float32)
            score_grad = (probs * (prob_grad - dot_head[block_pos][:, None]) * softmax_scale).astype(jnp.bfloat16)
            query_out.append(jnp.dot(score_grad, key_set, preferred_element_type=jnp.float32).astype(jnp.bfloat16))
            key_grad = jnp.dot(score_grad.T, query_head[block_pos], preferred_element_type=jnp.float32)
            key_acc = key_acc.at[chosen].add(key_grad.reshape(2, L, HD))
            value_acc = value_acc.at[chosen].add(value_grad.reshape(2, L, HD))
        return jnp.stack(query_out), key_acc.astype(jnp.bfloat16), value_acc.astype(jnp.bfloat16)

    grad_q, grad_k, grad_v = lax.map(one_head, (per_head(query), per_head(out_grad), row_dots, per_head(key_full), per_head(value_full)))
    return to_rows(grad_q), to_rows(grad_k), to_rows(grad_v)
```

```python
import jax
import jax.numpy as jnp
from jax import lax
from jax.experimental import pallas as pl
from jax.experimental.pallas import tpu as pltpu
from jax.sharding import PartitionSpec as P

HD = 128
SCALE = HD ** (-0.5)
LOG2E = 1.4426950408889634
PIECE = 32


def params(mib=56):
    return pltpu.CompilerParams(vmem_limit_bytes=mib << 20)


def pack(query, out_grad, forward_out, first, count, step, kv=None):
    _, toks, width = query.shape
    heads = width // HD
    blocks = kv[0].shape[0] if kv else 0
    slots = 2 * count + 1 + 2 * blocks
    steps = count // step
    start = first // step

    def body(*refs):
        q_ref, g_ref, f_ref = refs[:3]
        kv_refs = refs[3 : 3 + (4 if kv else 0)]
        out_ref = refs[3 + len(kv_refs)]
        dots, dots_out = refs[4 + len(kv_refs) : 6 + len(kv_refs)]
        kv_out = refs[6 + len(kv_refs)] if kv else None
        sems = refs[-1]
        at = pl.program_id(0)

        @pl.when(at == 0)
        def _():
            dots[...] = jnp.zeros_like(dots)
            if kv:
                for which in range(2):
                    codes, scales = kv_refs[2 * which], kv_refs[2 * which + 1]
                    factor = scales[...].astype(jnp.float32)
                    for h in range(heads):
                        part = codes[:, :, h * HD : (h + 1) * HD].astype(jnp.float32)
                        rows = part * factor[:, :, h : h + 1]
                        kv_out[h, which * blocks : (which + 1) * blocks] = rows.astype(jnp.bfloat16)

        for h in range(heads):
            pltpu.make_async_copy(
                q_ref.at[:, :, pl.ds(h * HD, HD)], out_ref.at[h, pl.ds(at * step, step)], sems.at[0]
            ).start()
            pltpu.make_async_copy(
                g_ref.at[:, :, pl.ds(h * HD, HD)],
                out_ref.at[h, pl.ds(count + at * step, step)],
                sems.at[1],
            ).start()
        lane = lax.broadcasted_iota(jnp.int32, (step, toks, HD), 2)
        place = lax.broadcasted_iota(jnp.int32, (step, toks, HD), 0) + at * step
        chosen = lane == place
        for h in range(heads):
            cut = slice(h * HD, (h + 1) * HD)
            product = g_ref[:, :, cut].astype(jnp.float32) * f_ref[:, :, cut].astype(jnp.float32)
            total = jnp.sum(product, axis=-1, keepdims=True)
            dots[h] += jnp.sum(jnp.where(chosen, total, 0.0), axis=0)

        @pl.when(at == steps - 1)
        def _():
            for h in range(heads):
                value = dots[h]
                high = value.astype(jnp.bfloat16).astype(jnp.float32)
                middle = (value - high).astype(jnp.bfloat16).astype(jnp.float32)
                low = (value - high - middle).astype(jnp.bfloat16).astype(jnp.float32)
                spread = high + pltpu.roll(middle, PIECE, 1) + pltpu.roll(low, 2 * PIECE, 1)
                dots_out[h, 0] = spread.astype(jnp.bfloat16)
            copies = [
                pltpu.make_async_copy(dots_out, out_ref.at[:, pl.ds(2 * count, 1)], sems.at[2])
            ]
            if kv:
                copies.append(
                    pltpu.make_async_copy(
                        kv_out, out_ref.at[:, pl.ds(2 * count + 1, 2 * blocks)], sems.at[3]
                    )
                )
            for copy in copies:
                copy.start()
            for copy in copies:
                copy.wait()

        pltpu.make_async_copy(q_ref, q_ref, sems.at[0]).wait()
        pltpu.make_async_copy(g_ref, g_ref, sems.at[1]).wait()

    rows = pl.BlockSpec((step, toks, width), lambda i: (start + i, 0, 0))
    in_specs = [rows] * 3
    args = [query, out_grad, forward_out]
    scratch = [
        pltpu.VMEM((heads, toks, HD), jnp.float32),
        pltpu.VMEM((heads, 1, toks, HD), jnp.bfloat16),
    ]
    if kv:
        in_specs += [pl.BlockSpec(x.shape, lambda i: (0, 0, 0)) for x in kv]
        args += list(kv)
        scratch.append(pltpu.VMEM((heads, 2 * blocks, toks, HD), jnp.bfloat16))
    scratch.append(pltpu.SemaphoreType.DMA((4,)))
    return pl.pallas_call(
        body,
        name=f"pack{first}",
        grid=(steps,),
        in_specs=in_specs,
        out_specs=pl.BlockSpec(memory_space=pl.ANY),
        out_shape=jax.ShapeDtypeStruct((heads, slots, toks, HD), jnp.bfloat16),
        scratch_shapes=scratch,
        compiler_params=params(),
    )(*args)


def nt(a, b):
    return lax.dot_general(a, b, (((1,), (1,)), ((), ())), preferred_element_type=jnp.float32)


def nn(a, b):
    return jnp.dot(a, b, preferred_element_type=jnp.float32)


def attend(pairs, message, kv_own, kv_other, first, count, sums=None, extra=0):
    srcs, slots, toks, _ = message.shape
    length = srcs * toks
    blocks = kv_own.shape[1] // 2
    total = 2 * blocks
    last = sums is not None

    def body(pair_ref, m_ref, own_ref, other_ref, *refs):
        if last:
            sum_ref, out_ref, own_sum, other_sum = refs[:4]
            keys, keys_t, values, dots, key_acc, value_acc = refs[4:]
        else:
            out_ref, sum_out = refs[:2]
            keys, keys_t, values, dots = refs[2:]
            key_acc, value_acc = sum_out.at[0], sum_out.at[1]
        for b in range(total):
            source, at = (own_ref, b) if b < blocks else (other_ref, b - blocks)
            key = source[:, at].reshape(length, HD)
            keys[b] = key
            keys_t[b] = key.astype(jnp.float32).T.astype(jnp.bfloat16)
            values[b] = source[:, blocks + at].reshape(length, HD)
        row = lax.broadcasted_iota(jnp.int32, (PIECE, HD), 0)
        lane = lax.broadcasted_iota(jnp.int32, (PIECE, HD), 1)
        picks = jnp.where((lane % PIECE == row) & (lane < 3 * PIECE), 1.0, 0.0).astype(jnp.bfloat16)
        dots[...] = nt(picks, m_ref[:, 2 * count].reshape(length, HD))
        if last:
            key_acc[...] = sum_ref[0]
            value_acc[...] = sum_ref[1]
        else:
            sum_out[...] = jnp.zeros_like(sum_out)

        def block(c):
            query = m_ref[:, c].reshape(length, HD)
            grad = m_ref[:, count + c].reshape(length, HD)
            dot_row = dots[pl.ds(c, 1), :]
            places = [pair_ref[2 * (first + c)], pair_ref[2 * (first + c) + 1]]
            scores = [nt(keys[b], query) * (SCALE * LOG2E) for b in places]
            high = jnp.maximum(
                jnp.max(scores[0], axis=0, keepdims=True), jnp.max(scores[1], axis=0, keepdims=True)
            )
            weights = [jnp.exp2(s - high) for s in scores]
            norm = jnp.sum(weights[0], axis=0, keepdims=True) + jnp.sum(
                weights[1], axis=0, keepdims=True
            )
            inverse = 1.0 / norm
            query_t = None
            for b, weight in zip(places, weights):
                probs = weight * inverse
                value_acc[b] += nn(probs.astype(jnp.bfloat16), grad)
                prob_grad = nt(values[b], grad)
                score_grad = (probs * (prob_grad - dot_row) * SCALE).astype(jnp.bfloat16)
                key_acc[b] += nn(score_grad, query)
                part = nn(keys_t[b], score_grad)
                query_t = part if query_t is None else query_t + part
            out_ref[:, c] = query_t.T.astype(jnp.bfloat16).reshape(srcs, toks, HD)

        lax.fori_loop(0, count, lambda c, _: (block(c), 0)[1], 0)
        if last:
            own_sum[0] = key_acc[:blocks]
            own_sum[1] = value_acc[:blocks]
            other_sum[0] = key_acc[blocks:].astype(jnp.bfloat16)
            other_sum[1] = value_acc[blocks:].astype(jnp.bfloat16)

    def whole(shape):
        return pl.BlockSpec(shape, lambda i, p: (0,) * len(shape))

    dq = jax.ShapeDtypeStruct((srcs, count + extra, toks, HD), jnp.bfloat16)
    dq_spec = whole((srcs, count, toks, HD))
    acc = (2, total, length, HD)
    scratch = [
        pltpu.VMEM((total, length, HD), jnp.bfloat16),
        pltpu.VMEM((total, HD, length), jnp.bfloat16),
        pltpu.VMEM((total, length, HD), jnp.bfloat16),
        pltpu.VMEM((PIECE, length), jnp.float32),
    ]
    in_specs = [whole(message.shape), whole(kv_own.shape), whole(kv_other.shape)]
    args = [message, kv_own, kv_other]
    if last:
        part = (2, blocks, length, HD)
        out_shape = (
            dq,
            jax.ShapeDtypeStruct(part, jnp.float32),
            jax.ShapeDtypeStruct(part, jnp.bfloat16),
        )
        out_specs = [dq_spec, whole(part), whole(part)]
        scratch += [pltpu.VMEM((total, length, HD), jnp.float32)] * 2
        in_specs.append(whole(acc))
        args.append(sums)
    else:
        out_shape = (dq, jax.ShapeDtypeStruct(acc, jnp.float32))
        out_specs = [dq_spec, whole(acc)]
    flops = 2 * 5 * count * length * 2 * length * HD
    return pl.pallas_call(
        body,
        name=f"attend{first}",
        grid_spec=pltpu.PrefetchScalarGridSpec(
            num_scalar_prefetch=1,
            grid=(1,),
            in_specs=in_specs,
            out_specs=out_specs,
            scratch_shapes=scratch,
        ),
        out_shape=out_shape,
        compiler_params=params(),
        cost_estimate=pl.CostEstimate(
            flops=flops, transcendentals=2 * count * length * length, bytes_accessed=6 << 20
        ),
    )(pairs, *args)


def combine(message, own_sum, other_sum, count):
    srcs, _, toks, _ = message.shape
    blocks = own_sum.shape[1]

    def body(_, own_ref, other_ref, out_ref):
        for b in range(blocks):
            value = own_ref[0, b] + other_ref[0, b].astype(jnp.float32)
            out_ref[:, b] = value.astype(jnp.bfloat16).reshape(srcs, toks, HD)

    part = pl.BlockSpec((1,) + own_sum.shape[1:], lambda i: (i, 0, 0, 0))
    return pl.pallas_call(
        body,
        name="combine",
        grid=(2,),
        in_specs=[pl.BlockSpec(memory_space=pl.ANY), part, part],
        out_specs=pl.BlockSpec(
            (srcs, blocks, toks, HD), lambda i: (0, count // blocks + i, 0, 0)
        ),
        out_shape=jax.ShapeDtypeStruct(message.shape, message.dtype),
        input_output_aliases={0: 0},
        compiler_params=params(),
    )(message, own_sum, other_sum)


def unpack(message, total, first, count, step, into=None, blocks=0):
    heads, slots, toks, _ = message.shape
    width = heads * HD
    start = first // step

    def body(*refs):
        m_ref = refs[0]
        refs = refs[1:]
        if blocks:
            kv_refs, refs = refs[:2], refs[2:]
        if into is not None:
            refs = refs[1:]
        out_ref = refs[0]
        for h in range(heads):
            out_ref[:, :, h * HD : (h + 1) * HD] = m_ref[h]
        if blocks:

            @pl.when(pl.program_id(0) == 0)
            def _():
                for source, target in zip(kv_refs, refs[1:]):
                    for h in range(heads):
                        target[:, :, h * HD : (h + 1) * HD] = source[h]

    in_specs = [pl.BlockSpec((heads, step, toks, HD), lambda i: (0, i, 0, 0))]
    args = [message]
    out_shape = [jax.ShapeDtypeStruct((total, toks, width), message.dtype)]
    out_specs = [pl.BlockSpec((step, toks, width), lambda i: (start + i, 0, 0))]
    if blocks:
        behind = count // blocks
        in_specs += [
            pl.BlockSpec((heads, blocks, toks, HD), lambda i: (0, behind, 0, 0)),
            pl.BlockSpec((heads, blocks, toks, HD), lambda i: (0, behind + 1, 0, 0)),
        ]
        args += [message] * 2
        out_shape += [jax.ShapeDtypeStruct((blocks, toks, width), message.dtype)] * 2
        out_specs += [pl.BlockSpec((blocks, toks, width), lambda i: (0, 0, 0))] * 2
    aliases = {}
    if into is not None:
        in_specs.append(pl.BlockSpec(memory_space=pl.ANY))
        aliases = {len(args): 0}
        args.append(into)
    return pl.pallas_call(
        body,
        name=f"unpack{first}",
        grid=(count // step,),
        in_specs=in_specs,
        out_specs=out_specs,
        out_shape=out_shape,
        input_output_aliases=aliases,
        compiler_params=params(),
    )(*args)


def to_heads(message):
    return lax.all_to_all(message, "head", split_axis=0, concat_axis=0, tiled=True)


def on_device(
    query, out_grad, forward_out, key_codes, key_scale, value_codes, value_scale, pairing
):
    count = query.shape[0]
    blocks = key_codes.shape[0]
    half = count // 2
    swap = [(0, 1), (1, 0)]
    group = lax.axis_index("grp")
    mine = lax.dynamic_slice_in_dim(pairing, group * count, count, 0)
    pairs = ((mine + blocks * group) % (2 * blocks)).reshape(-1)

    send0 = pack(
        query, out_grad, forward_out, 0, half, 6, (key_codes, key_scale, value_codes, value_scale)
    )
    got0 = to_heads(send0)
    send1 = pack(query, out_grad, forward_out, half, half, 6)
    got1 = to_heads(send1)
    kv_own = got0[:, 2 * half + 1 :]
    kv_other = lax.ppermute(kv_own, "grp", swap)
    grad0, sums = attend(pairs, got0, kv_own, kv_other, 0, half)
    back0 = to_heads(grad0)
    grad1, own_sum, other_sum = attend(
        pairs, got1, kv_own, kv_other, half, half, sums, extra=2 * blocks
    )
    theirs = lax.ppermute(other_sum, "grp", swap)
    grad1 = combine(grad1, own_sum, theirs, half)
    back1 = to_heads(grad1)
    (rows,) = unpack(back0, count, 0, half, 6)
    rows, key_rows, value_rows = unpack(back1, count, half, half, 6, into=rows, blocks=blocks)
    return rows, key_rows, value_rows


def solution(mesh):
    spec = P("grp", "head", None)
    return jax.shard_map(
        on_device,
        mesh=mesh,
        in_specs=(spec,) * 7 + (P(),),
        out_specs=(spec,) * 3,
        check_vma=False,
    )
```

```python
import jax
import jax.numpy as jnp
from jax import lax
from jax.experimental import pallas as pl
from jax.experimental.pallas import tpu as pltpu
from jax.sharding import PartitionSpec as P


HD = 128
SCALE = HD ** (-0.5)
LOG2E = 1.4426950408889634
EXP_SCALE = SCALE * LOG2E
SLOTS = 3
PIECE = 32


def params(mib=56):
    return pltpu.CompilerParams(vmem_limit_bytes=mib << 20)


def pack(query, out_grad, forward_out, first, count, step, kv=None):
    _, toks, width = query.shape
    heads = width // HD
    blocks = kv[0].shape[0] if kv else 0
    slots = 2 * count + 1 + 2 * blocks
    steps = count // step
    start = first // step

    def body(*refs):
        q_ref, g_ref, f_ref = refs[:3]
        kv_refs = refs[3 : 3 + (4 if kv else 0)]
        out_ref = refs[3 + len(kv_refs)]
        dots, dots_out = refs[4 + len(kv_refs) : 6 + len(kv_refs)]
        kv_out = refs[6 + len(kv_refs)] if kv else None
        sems = refs[-1]
        at = pl.program_id(0)

        @pl.when(at == 0)
        def _():
            dots[...] = jnp.zeros_like(dots)
            if kv:
                for which in range(2):
                    codes, scales = kv_refs[2 * which], kv_refs[2 * which + 1]
                    factor = scales[...].astype(jnp.float32)
                    for h in range(heads):
                        part = codes[:, :, h * HD : (h + 1) * HD].astype(jnp.float32)
                        rows = part * factor[:, :, h : h + 1]
                        kv_out[h, which * blocks : (which + 1) * blocks] = rows.astype(jnp.bfloat16)

        for h in range(heads):
            pltpu.make_async_copy(
                q_ref.at[:, :, pl.ds(h * HD, HD)], out_ref.at[h, pl.ds(at * step, step)], sems.at[0]
            ).start()
            pltpu.make_async_copy(
                g_ref.at[:, :, pl.ds(h * HD, HD)],
                out_ref.at[h, pl.ds(count + at * step, step)],
                sems.at[1],
            ).start()
        lane = lax.broadcasted_iota(jnp.int32, (step, toks, HD), 2)
        place = lax.broadcasted_iota(jnp.int32, (step, toks, HD), 0) + at * step
        chosen = lane == place
        for h in range(heads):
            cut = slice(h * HD, (h + 1) * HD)
            product = g_ref[:, :, cut].astype(jnp.float32) * f_ref[:, :, cut].astype(jnp.float32)
            total = jnp.sum(product, axis=-1, keepdims=True)
            dots[h] += jnp.sum(jnp.where(chosen, total, 0.0), axis=0)

        @pl.when(at == steps - 1)
        def _():
            for h in range(heads):
                value = dots[h]
                high = value.astype(jnp.bfloat16).astype(jnp.float32)
                middle = (value - high).astype(jnp.bfloat16).astype(jnp.float32)
                low = (value - high - middle).astype(jnp.bfloat16).astype(jnp.float32)
                spread = high + pltpu.roll(middle, PIECE, 1) + pltpu.roll(low, 2 * PIECE, 1)
                dots_out[h, 0] = spread.astype(jnp.bfloat16)
            copies = [
                pltpu.make_async_copy(dots_out, out_ref.at[:, pl.ds(2 * count, 1)], sems.at[2])
            ]
            if kv:
                copies.append(
                    pltpu.make_async_copy(
                        kv_out, out_ref.at[:, pl.ds(2 * count + 1, 2 * blocks)], sems.at[3]
                    )
                )
            for copy in copies:
                copy.start()
            for copy in copies:
                copy.wait()

        pltpu.make_async_copy(q_ref, q_ref, sems.at[0]).wait()
        pltpu.make_async_copy(g_ref, g_ref, sems.at[1]).wait()

    rows = pl.BlockSpec((step, toks, width), lambda i: (start + i, 0, 0))
    in_specs = [rows] * 3
    args = [query, out_grad, forward_out]
    scratch = [
        pltpu.VMEM((heads, toks, HD), jnp.float32),
        pltpu.VMEM((heads, 1, toks, HD), jnp.bfloat16),
    ]
    if kv:
        in_specs += [pl.BlockSpec(x.shape, lambda i: (0, 0, 0)) for x in kv]
        args += list(kv)
        scratch.append(pltpu.VMEM((heads, 2 * blocks, toks, HD), jnp.bfloat16))
    scratch.append(pltpu.SemaphoreType.DMA((4,)))
    return pl.pallas_call(
        body,
        grid=(steps,),
        in_specs=in_specs,
        out_specs=pl.BlockSpec(memory_space=pl.ANY),
        out_shape=jax.ShapeDtypeStruct((heads, slots, toks, HD), jnp.bfloat16),
        scratch_shapes=scratch,
        compiler_params=params(),
    )(*args)


def nt(a, b):
    return lax.dot_general(a, b, (((1,), (1,)), ((), ())), preferred_element_type=jnp.float32)


def nn(a, b):
    return jnp.dot(a, b, preferred_element_type=jnp.float32)


def attend(pairs, message, kv_own, kv_other, first, count, total_out, sums=None, into=None):
    srcs, _, toks, _ = message.shape
    length = srcs * toks
    blocks = kv_own.shape[1] // 2
    total = 2 * blocks
    last = sums is not None

    def body(pair_ref, m_ref, own_ref, other_ref, *refs):
        if last:
            sum_ref, _, target = refs[:3]
            refs, (key_acc, value_acc, out_ref, sems) = refs[3:-4], refs[-4:]
        else:
            out_ref, sum_out = refs[:2]
            refs = refs[2:]
            key_acc, value_acc = sum_out.at[0], sum_out.at[1]
        keys, keys_t, values, dots = refs[:4]
        scores, prob_grads, probs, score_grads, queries, grads = (
            refs[4 + SLOTS * at : 4 + SLOTS * (at + 1)] for at in range(6)
        )
        for b in range(total):
            source, at = (own_ref, b) if b < blocks else (other_ref, b - blocks)
            key = source[:, at].reshape(length, HD)
            keys[b] = key
            keys_t[b] = key.astype(jnp.float32).T.astype(jnp.bfloat16)
            values[b] = source[:, blocks + at].reshape(length, HD)
        row = lax.broadcasted_iota(jnp.int32, (PIECE, HD), 0)
        lane = lax.broadcasted_iota(jnp.int32, (PIECE, HD), 1)
        picks = jnp.where((lane % PIECE == row) & (lane < 3 * PIECE), 1.0, 0.0).astype(jnp.bfloat16)
        dots[...] = nt(picks, m_ref[:, 2 * count].reshape(length, HD))
        if last:
            key_acc[...] = sum_ref[0]
            value_acc[...] = sum_ref[1]
        else:
            sum_out[...] = jnp.zeros_like(sum_out)

        def place(c, j):
            return pair_ref[2 * (first + c) + j]

        def scores_of(c, slot):
            query = m_ref[:, c].reshape(length, HD)
            grad = m_ref[:, count + c].reshape(length, HD)
            queries[slot][...] = query
            grads[slot][...] = grad
            for j in range(2):
                scores[slot][j] = nt(keys[place(c, j)], query)
                prob_grads[slot][j] = nt(values[place(c, j)], grad)

        def probs_of(c, slot):
            score, prob_grad = scores[slot], prob_grads[slot]
            cuts = [(j, slice(r, r + 32)) for j in range(2) for r in range(0, length, 32)]
            high = None
            for j, rows in cuts:
                part = jnp.max(score[j, rows].reshape(32 // 8, 8, length), axis=0)
                high = part if high is None else jnp.maximum(high, part)
            high = jnp.max(high, axis=0, keepdims=True) * EXP_SCALE
            norm = None
            for j, rows in cuts:
                weight = jnp.exp2(score[j, rows] * EXP_SCALE - high)
                score[j, rows] = weight
                part = jnp.sum(weight.reshape(32 // 8, 8, length), axis=0)
                norm = part if norm is None else norm + part
            inverse = 1.0 / jnp.sum(norm, axis=0, keepdims=True)
            dot_row = dots[pl.ds(c, 1), :]
            for j, rows in cuts:
                prob = score[j, rows] * inverse
                probs[slot][j, rows] = prob.astype(jnp.bfloat16)
                score_grads[slot][j, rows] = (prob * (prob_grad[j, rows] - dot_row)).astype(
                    jnp.bfloat16
                )

        def grads_of(c, slot):
            query_t = None
            for j in range(2):
                b = place(c, j)
                value_acc[b] += nn(probs[slot][j], grads[slot][...])
                key_acc[b] += nn(score_grads[slot][j], queries[slot][...])
                part = nn(keys_t[b], score_grads[slot][j])
                query_t = part if query_t is None else query_t + part
            out_ref[:, c] = (query_t * SCALE).T.astype(jnp.bfloat16).reshape(srcs, toks, HD)

        for ref in (probs[-1], score_grads[-1], queries[-1], grads[-1]):
            ref[...] = jnp.zeros_like(ref)
        scores_of(0, 0)

        def several(i, _):
            for k in range(SLOTS):
                c = i * SLOTS + k
                grads_of(jnp.maximum(c - 1, 0), (k - 1) % SLOTS)
                scores_of(jnp.minimum(c + 1, count - 1), (k + 1) % SLOTS)
                probs_of(c, k)
            return 0

        lax.fori_loop(0, count // SLOTS, several, 0)
        grads_of(count - 1, SLOTS - 1)
        if last:
            for b in range(total):
                at = count + (b // blocks) * 2 * blocks + b % blocks
                key_rows = (key_acc[b] * SCALE).astype(jnp.bfloat16)
                out_ref[:, at] = key_rows.reshape(srcs, toks, HD)
                value_rows = value_acc[b].astype(jnp.bfloat16)
                out_ref[:, at + blocks] = value_rows.reshape(srcs, toks, HD)
            copy = pltpu.make_async_copy(
                out_ref, target.at[:, pl.ds(first, count + 2 * total)], sems.at[0]
            )
            copy.start()
            copy.wait()

    def whole(shape):
        return pl.BlockSpec(shape, lambda i, p: (0,) * len(shape))

    dq = jax.ShapeDtypeStruct((srcs, total_out, toks, HD), jnp.bfloat16)
    dq_spec = whole((srcs, count, toks, HD))
    acc = (2, total, length, HD)
    scratch = [
        pltpu.VMEM((total, length, HD), jnp.bfloat16),
        pltpu.VMEM((total, HD, length), jnp.bfloat16),
        pltpu.VMEM((total, length, HD), jnp.bfloat16),
        pltpu.VMEM((PIECE, length), jnp.float32),
    ]
    scratch += [pltpu.VMEM((2, length, length), jnp.float32)] * (2 * SLOTS)
    scratch += [pltpu.VMEM((2, length, length), jnp.bfloat16)] * (2 * SLOTS)
    scratch += [pltpu.VMEM((length, HD), jnp.bfloat16)] * (2 * SLOTS)
    in_specs = [whole(message.shape), whole(kv_own.shape), whole(kv_other.shape)]
    args = [message, kv_own, kv_other]
    aliases = {}
    if last:
        out_shape = dq
        out_specs = pl.BlockSpec(memory_space=pl.ANY)
        scratch += [pltpu.VMEM((total, length, HD), jnp.float32)] * 2
        scratch.append(pltpu.VMEM((srcs, count + 2 * total, toks, HD), jnp.bfloat16))
        scratch.append(pltpu.SemaphoreType.DMA((1,)))
        in_specs += [whole(acc), pl.BlockSpec(memory_space=pl.ANY)]
        args += [sums, into]
        aliases = {len(args): 0}
    else:
        out_shape = (dq, jax.ShapeDtypeStruct(acc, jnp.float32))
        out_specs = [dq_spec, whole(acc)]
    flops = 2 * 5 * count * length * 2 * length * HD
    return pl.pallas_call(
        body,
        grid_spec=pltpu.PrefetchScalarGridSpec(
            num_scalar_prefetch=1,
            grid=(1,),
            in_specs=in_specs,
            out_specs=out_specs,
            scratch_shapes=scratch,
        ),
        out_shape=out_shape,
        input_output_aliases=aliases,
        compiler_params=params(),
        cost_estimate=pl.CostEstimate(
            flops=flops, transcendentals=2 * count * length * length, bytes_accessed=6 << 20
        ),
    )(pairs, *args)


def unpack(message, count, step):
    heads, _, toks, _ = message.shape
    width = heads * HD

    def body(m_ref, out_ref):
        for h in range(heads):
            out_ref[:, :, h * HD : (h + 1) * HD] = m_ref[h]

    return pl.pallas_call(
        body,
        name="unpack",
        grid=(count // step,),
        in_specs=[pl.BlockSpec((heads, step, toks, HD), lambda i: (0, i, 0, 0))],
        out_specs=pl.BlockSpec((step, toks, width), lambda i: (i, 0, 0)),
        out_shape=jax.ShapeDtypeStruct((count, toks, width), message.dtype),
        compiler_params=params(),
    )(message)


def unpack_sums(message, theirs, first, blocks):
    heads, _, toks, _ = message.shape
    width = heads * HD
    behind = first // blocks

    def body(k_ref, v_ref, t_ref, key_out, value_out):
        for which, (mine, out) in enumerate(((k_ref, key_out), (v_ref, value_out))):
            for h in range(heads):
                other = t_ref[h, which * blocks : (which + 1) * blocks].astype(jnp.float32)
                total = mine[h].astype(jnp.float32) + other
                out[:, :, h * HD : (h + 1) * HD] = total.astype(jnp.bfloat16)

    rows = jax.ShapeDtypeStruct((blocks, toks, width), message.dtype)
    rows_spec = pl.BlockSpec((blocks, toks, width), lambda i: (0, 0, 0))
    return pl.pallas_call(
        body,
        name="unpack_sums",
        grid=(1,),
        in_specs=[
            pl.BlockSpec((heads, blocks, toks, HD), lambda i: (0, behind, 0, 0)),
            pl.BlockSpec((heads, blocks, toks, HD), lambda i: (0, behind + 1, 0, 0)),
            pl.BlockSpec(theirs.shape, lambda i: (0, 0, 0, 0)),
        ],
        out_specs=[rows_spec] * 2,
        out_shape=[rows] * 2,
        compiler_params=params(),
    )(message, message, theirs)


def to_heads(message):
    return lax.all_to_all(message, "head", split_axis=0, concat_axis=0, tiled=True)


def on_device(
    query, out_grad, forward_out, key_codes, key_scale, value_codes, value_scale, pairing
):
    count = query.shape[0]
    blocks = key_codes.shape[0]
    large = count * 2 // 3
    small = count - large
    swap = [(0, 1), (1, 0)]
    group = lax.axis_index("grp")
    mine = lax.dynamic_slice_in_dim(pairing, group * count, count, 0)
    pairs = ((mine + blocks * group) % (2 * blocks)).reshape(-1)
    codes = (key_codes, key_scale, value_codes, value_scale)
    send0 = pack(query, out_grad, forward_out, 0, large, 6, codes)
    got0 = to_heads(send0)
    send1 = pack(query, out_grad, forward_out, large, small, 6)
    got1 = to_heads(send1)
    kv_own = got0[:, 2 * large + 1 :]
    kv_other = lax.ppermute(kv_own, "grp", swap)
    slots = count + 4 * blocks
    grads, sums = attend(pairs, got0, kv_own, kv_other, 0, large, slots)
    grads = attend(pairs, got1, kv_own, kv_other, large, small, slots, sums, grads)
    back = to_heads(grads)
    theirs = lax.ppermute(back[:, count + 2 * blocks :], "grp", swap)
    rows = unpack(back, count, 6)
    key_rows, value_rows = unpack_sums(back, theirs, count, blocks)
    return rows, key_rows, value_rows


def solution(mesh):
    spec = P("grp", "head", None)
    return jax.shard_map(
        on_device,
        mesh=mesh,
        in_specs=(spec,) * 7 + (P(),),
        out_specs=(spec,) * 3,
        check_vma=False,
    )
```

```python
import jax
import jax.numpy as jnp
from jax import lax
from jax.experimental import pallas as pl
from jax.experimental.pallas import tpu as pltpu
from jax.sharding import PartitionSpec as P


HD = 128
SCALE = HD ** (-0.5)
LOG2E = 1.4426950408889634
EXP_SCALE = SCALE * LOG2E
SLOTS = 3
PIECE = 32


HELD = pl.BlockSpec(memory_space=pltpu.VMEM)


def held(x):
    return pltpu.with_memory_space_constraint(x, pltpu.VMEM)


def params(mib=56):
    return pltpu.CompilerParams(vmem_limit_bytes=mib << 20)


def pack(query, out_grad, forward_out, first, count, step, kv=None):
    _, toks, width = query.shape
    heads = width // HD
    blocks = kv[0].shape[0] if kv else 0
    slots = 2 * count + 1 + 2 * blocks
    steps = count // step
    start = first // step

    def body(*refs):
        q_ref, g_ref, f_ref = refs[:3]
        kv_refs = refs[3 : 3 + (4 if kv else 0)]
        out_ref = refs[3 + len(kv_refs)]
        dots, dots_out = refs[4 + len(kv_refs) : 6 + len(kv_refs)]
        kv_out = refs[6 + len(kv_refs)] if kv else None
        sems = refs[-1]
        at = pl.program_id(0)

        @pl.when(at == 0)
        def _():
            dots[...] = jnp.zeros_like(dots)
            if kv:
                for which in range(2):
                    codes, scales = kv_refs[2 * which], kv_refs[2 * which + 1]
                    factor = scales[...].astype(jnp.float32)
                    for h in range(heads):
                        part = codes[:, :, h * HD : (h + 1) * HD].astype(jnp.float32)
                        rows = part * factor[:, :, h : h + 1]
                        kv_out[h, which * blocks : (which + 1) * blocks] = rows.astype(jnp.bfloat16)

        for h in range(heads):
            pltpu.make_async_copy(
                q_ref.at[:, :, pl.ds(h * HD, HD)], out_ref.at[h, pl.ds(at * step, step)], sems.at[0]
            ).start()
            pltpu.make_async_copy(
                g_ref.at[:, :, pl.ds(h * HD, HD)],
                out_ref.at[h, pl.ds(count + at * step, step)],
                sems.at[1],
            ).start()
        lane = lax.broadcasted_iota(jnp.int32, (step * toks, HD), 1)
        place = lax.broadcasted_iota(jnp.int32, (step * toks, HD), 0) // toks + at * step
        chosen = lane == place
        for h in range(heads):
            cut = slice(h * HD, (h + 1) * HD)
            product = g_ref[:, :, cut].astype(jnp.float32) * f_ref[:, :, cut].astype(jnp.float32)
            total = jnp.sum(product.reshape(step * toks, HD), axis=-1, keepdims=True)
            rows_of = jnp.where(chosen, total, 0.0)
            dots[h] += jnp.sum(rows_of.reshape(step, toks, HD), axis=0)

        @pl.when(at == steps - 1)
        def _():
            for h in range(heads):
                value = dots[h]
                high = value.astype(jnp.bfloat16).astype(jnp.float32)
                middle = (value - high).astype(jnp.bfloat16).astype(jnp.float32)
                low = (value - high - middle).astype(jnp.bfloat16).astype(jnp.float32)
                spread = high + pltpu.roll(middle, PIECE, 1) + pltpu.roll(low, 2 * PIECE, 1)
                dots_out[h, 0] = spread.astype(jnp.bfloat16)
            copies = [
                pltpu.make_async_copy(dots_out, out_ref.at[:, pl.ds(2 * count, 1)], sems.at[2])
            ]
            if kv:
                copies.append(
                    pltpu.make_async_copy(
                        kv_out, out_ref.at[:, pl.ds(2 * count + 1, 2 * blocks)], sems.at[3]
                    )
                )
            for copy in copies:
                copy.start()
            for copy in copies:
                copy.wait()

        pltpu.make_async_copy(q_ref, q_ref, sems.at[0]).wait()
        pltpu.make_async_copy(g_ref, g_ref, sems.at[1]).wait()

    rows = pl.BlockSpec((step, toks, width), lambda i: (start + i, 0, 0))
    in_specs = [rows] * 3
    args = [query, out_grad, forward_out]
    scratch = [
        pltpu.VMEM((heads, toks, HD), jnp.float32),
        pltpu.VMEM((heads, 1, toks, HD), jnp.bfloat16),
    ]
    if kv:
        in_specs += [pl.BlockSpec(x.shape, lambda i: (0, 0, 0)) for x in kv]
        args += list(kv)
        scratch.append(pltpu.VMEM((heads, 2 * blocks, toks, HD), jnp.bfloat16))
    scratch.append(pltpu.SemaphoreType.DMA((4,)))
    return pl.pallas_call(
        body,
        grid=(steps,),
        in_specs=in_specs,
        out_specs=pl.BlockSpec(memory_space=pl.ANY),
        out_shape=jax.ShapeDtypeStruct((heads, slots, toks, HD), jnp.bfloat16),
        scratch_shapes=scratch,
        compiler_params=params(),
    )(*args)


def nt(a, b):
    return lax.dot_general(a, b, (((1,), (1,)), ((), ())), preferred_element_type=jnp.float32)


def nn(a, b):
    return jnp.dot(a, b, preferred_element_type=jnp.float32)


def attend(pairs, message, kv_own, kv_other, first, count, total_out, sums=None, into=None):
    srcs, _, toks, _ = message.shape
    length = srcs * toks
    blocks = kv_own.shape[1] // 2
    total = 2 * blocks
    last = sums is not None

    def body(pair_ref, m_ref, own_ref, other_ref, *refs):
        if last:
            sum_ref, _, target = refs[:3]
            refs, (key_acc, value_acc, out_ref, sems) = refs[3:-4], refs[-4:]
        else:
            out_ref, sum_out = refs[:2]
            refs = refs[2:]
            key_acc, value_acc = sum_out.at[0], sum_out.at[1]
        keys, keys_t, values, dots = refs[:4]
        scores, prob_grads, probs, score_grads, queries, grads = (
            refs[4 + SLOTS * at : 4 + SLOTS * (at + 1)] for at in range(6)
        )
        for b in range(total):
            source, at = (own_ref, b) if b < blocks else (other_ref, b - blocks)
            key = source[:, at].reshape(length, HD)
            keys[b] = key
            keys_t[b] = key.astype(jnp.float32).T.astype(jnp.bfloat16)
            values[b] = source[:, blocks + at].reshape(length, HD)
        row = lax.broadcasted_iota(jnp.int32, (PIECE, HD), 0)
        lane = lax.broadcasted_iota(jnp.int32, (PIECE, HD), 1)
        picks = jnp.where((lane % PIECE == row) & (lane < 3 * PIECE), 1.0, 0.0).astype(jnp.bfloat16)
        dots[...] = nt(picks, m_ref[:, 2 * count].reshape(length, HD))
        if last:
            key_acc[...] = sum_ref[0]
            value_acc[...] = sum_ref[1]
        else:
            sum_out[...] = jnp.zeros_like(sum_out)

        def place(c, j):
            return pair_ref[2 * (first + c) + j]

        def scores_of(c, slot):
            query = m_ref[:, c].reshape(length, HD)
            grad = m_ref[:, count + c].reshape(length, HD)
            queries[slot][...] = query
            grads[slot][...] = grad
            for j in range(2):
                scores[slot][j] = nt(keys[place(c, j)], query)
                prob_grads[slot][j] = nt(values[place(c, j)], grad)

        def probs_of(c, slot):
            score, prob_grad = scores[slot], prob_grads[slot]
            cuts = [(j, slice(r, r + 32)) for j in range(2) for r in range(0, length, 32)]
            high = None
            for j, rows in cuts:
                part = jnp.max(score[j, rows].reshape(32 // 8, 8, length), axis=0)
                high = part if high is None else jnp.maximum(high, part)
            high = jnp.max(high, axis=0, keepdims=True) * EXP_SCALE
            norm = None
            for j, rows in cuts:
                weight = jnp.exp2(score[j, rows] * EXP_SCALE - high)
                score[j, rows] = weight
                part = jnp.sum(weight.reshape(32 // 8, 8, length), axis=0)
                norm = part if norm is None else norm + part
            inverse = 1.0 / jnp.sum(norm, axis=0, keepdims=True)
            dot_row = dots[pl.ds(c, 1), :]
            for j, rows in cuts:
                prob = score[j, rows] * inverse
                probs[slot][j, rows] = prob.astype(jnp.bfloat16)
                score_grads[slot][j, rows] = (prob * (prob_grad[j, rows] - dot_row)).astype(
                    jnp.bfloat16
                )

        def grads_of(c, slot):
            query_t = None
            for j in range(2):
                b = place(c, j)
                value_acc[b] += nn(probs[slot][j], grads[slot][...])
                key_acc[b] += nn(score_grads[slot][j], queries[slot][...])
                part = nn(keys_t[b], score_grads[slot][j])
                query_t = part if query_t is None else query_t + part
            out_ref[:, c] = (query_t * SCALE).T.astype(jnp.bfloat16).reshape(srcs, toks, HD)

        for ref in (probs[-1], score_grads[-1], queries[-1], grads[-1]):
            ref[...] = jnp.zeros_like(ref)
        scores_of(0, 0)

        def several(i, _):
            for k in range(SLOTS):
                c = i * SLOTS + k
                grads_of(jnp.maximum(c - 1, 0), (k - 1) % SLOTS)
                scores_of(jnp.minimum(c + 1, count - 1), (k + 1) % SLOTS)
                probs_of(c, k)
            return 0

        lax.fori_loop(0, count // SLOTS, several, 0)
        grads_of(count - 1, SLOTS - 1)
        if last:
            for b in range(total):
                at = count + (b // blocks) * 2 * blocks + b % blocks
                key_rows = (key_acc[b] * SCALE).astype(jnp.bfloat16)
                out_ref[:, at] = key_rows.reshape(srcs, toks, HD)
                value_rows = value_acc[b].astype(jnp.bfloat16)
                out_ref[:, at + blocks] = value_rows.reshape(srcs, toks, HD)
            copy = pltpu.make_async_copy(
                out_ref, target.at[:, pl.ds(first, count + 2 * total)], sems.at[0]
            )
            copy.start()
            copy.wait()

    def whole(shape):
        return pl.BlockSpec(shape, lambda i, p: (0,) * len(shape))

    dq = jax.ShapeDtypeStruct((srcs, total_out, toks, HD), jnp.bfloat16)
    dq_spec = whole((srcs, count, toks, HD))
    acc = (2, total, length, HD)
    scratch = [
        pltpu.VMEM((total, length, HD), jnp.bfloat16),
        pltpu.VMEM((total, HD, length), jnp.bfloat16),
        pltpu.VMEM((total, length, HD), jnp.bfloat16),
        pltpu.VMEM((PIECE, length), jnp.float32),
    ]
    scratch += [pltpu.VMEM((2, length, length), jnp.float32)] * (2 * SLOTS)
    scratch += [pltpu.VMEM((2, length, length), jnp.bfloat16)] * (2 * SLOTS)
    scratch += [pltpu.VMEM((length, HD), jnp.bfloat16)] * (2 * SLOTS)
    in_specs = [HELD if last else whole(message.shape), HELD, HELD]
    args = [held(message) if last else message, held(kv_own), held(kv_other)]
    aliases = {}
    if last:
        out_shape = dq
        out_specs = pl.BlockSpec(memory_space=pl.ANY)
        scratch += [pltpu.VMEM((total, length, HD), jnp.float32)] * 2
        scratch.append(pltpu.VMEM((srcs, count + 2 * total, toks, HD), jnp.bfloat16))
        scratch.append(pltpu.SemaphoreType.DMA((1,)))
        in_specs += [HELD, pl.BlockSpec(memory_space=pl.ANY)]
        args += [held(sums), into]
        aliases = {len(args): 0}
    else:
        out_shape = (dq, pltpu.VMEM(acc, jnp.float32))
        out_specs = [dq_spec, HELD]
    flops = 2 * 5 * count * length * 2 * length * HD
    return pl.pallas_call(
        body,
        grid_spec=pltpu.PrefetchScalarGridSpec(
            num_scalar_prefetch=1,
            grid=(1,),
            in_specs=in_specs,
            out_specs=out_specs,
            scratch_shapes=scratch,
        ),
        out_shape=out_shape,
        input_output_aliases=aliases,
        compiler_params=params(),
        cost_estimate=pl.CostEstimate(
            flops=flops, transcendentals=2 * count * length * length, bytes_accessed=6 << 20
        ),
    )(pairs, *args)


def unpack(message, count, step):
    heads, _, toks, _ = message.shape
    width = heads * HD

    def body(m_ref, out_ref):
        first = pl.program_id(0) * step
        for h in range(heads):
            out_ref[:, :, h * HD : (h + 1) * HD] = m_ref[h, pl.ds(first, step)]

    return pl.pallas_call(
        body,
        name="unpack",
        grid=(count // step,),
        in_specs=[HELD],
        out_specs=pl.BlockSpec((step, toks, width), lambda i: (i, 0, 0)),
        out_shape=jax.ShapeDtypeStruct((count, toks, width), message.dtype),
        compiler_params=params(),
    )(held(message))


def unpack_sums(message, theirs, first, blocks):
    heads, _, toks, _ = message.shape
    width = heads * HD

    def body(m_ref, t_ref, *outs):
        for which, out in enumerate(outs):
            at = which * blocks
            for h in range(heads):
                total = m_ref[h, first + at : first + at + blocks].astype(jnp.float32)
                total += t_ref[h, at : at + blocks].astype(jnp.float32)
                out[:, :, h * HD : (h + 1) * HD] = total.astype(jnp.bfloat16)

    rows = jax.ShapeDtypeStruct((blocks, toks, width), message.dtype)
    return pl.pallas_call(
        body,
        name="unpack_sums",
        grid=(1,),
        in_specs=[HELD] * 2,
        out_specs=[pl.BlockSpec((blocks, toks, width), lambda i: (0, 0, 0))] * 2,
        out_shape=[rows] * 2,
        compiler_params=params(),
    )(held(message), held(theirs))


def to_heads(message):
    return lax.all_to_all(message, "head", split_axis=0, concat_axis=0, tiled=True)


def on_device(
    query, out_grad, forward_out, key_codes, key_scale, value_codes, value_scale, pairing
):
    count = query.shape[0]
    blocks = key_codes.shape[0]
    large = count * 3 // 4
    small = count - large
    swap = [(0, 1), (1, 0)]
    group = lax.axis_index("grp")
    mine = lax.dynamic_slice_in_dim(pairing, group * count, count, 0)
    pairs = ((mine + blocks * group) % (2 * blocks)).reshape(-1)
    codes = (key_codes, key_scale, value_codes, value_scale)
    send0 = pack(query, out_grad, forward_out, 0, large, large, codes)
    got0 = to_heads(send0)
    send1 = pack(query, out_grad, forward_out, large, small, small)
    got1 = to_heads(send1)
    kv_own = got0[:, 2 * large + 1 :]
    kv_other = lax.ppermute(kv_own, "grp", swap)
    slots = count + 4 * blocks
    grads, sums = attend(pairs, got0, kv_own, kv_other, 0, large, slots)
    grads = attend(pairs, got1, kv_own, kv_other, large, small, slots, sums, grads)
    back = to_heads(grads)
    theirs = lax.ppermute(back[:, count + 2 * blocks :], "grp", swap)
    rows = unpack(back, count, 6)
    key_rows, value_rows = unpack_sums(back, theirs, count, blocks)
    return rows, key_rows, value_rows


def solution(mesh):
    spec = P("grp", "head", None)
    return jax.shard_map(
        on_device,
        mesh=mesh,
        in_specs=(spec,) * 7 + (P(),),
        out_specs=(spec,) * 3,
        check_vma=False,
    )
```

```python
import jax
import jax.numpy as jnp
from jax import lax
from jax.experimental import pallas as pl
from jax.experimental.pallas import tpu as pltpu
from jax.sharding import PartitionSpec as P


HD = 128
SCALE = HD ** (-0.5)
LOG2E = 1.4426950408889634
EXP_SCALE = SCALE * LOG2E
SLOTS = 3
PIECE = 32


HELD = pl.BlockSpec(memory_space=pltpu.VMEM)


def held(x):
    return pltpu.with_memory_space_constraint(x, pltpu.VMEM)


def params(mib=56):
    return pltpu.CompilerParams(vmem_limit_bytes=mib << 20)


def pack(query, out_grad, forward_out, first, count, step, kv=None):
    _, toks, width = query.shape
    heads = width // HD
    blocks = kv[0].shape[0] if kv else 0
    slots = 2 * count + 1 + 2 * blocks
    steps = count // step
    start = first // step

    def body(*refs):
        q_ref, g_ref, f_ref = refs[:3]
        kv_refs = refs[3 : 3 + (4 if kv else 0)]
        out_ref = refs[3 + len(kv_refs)]
        dots, dots_out = refs[4 + len(kv_refs) : 6 + len(kv_refs)]
        kv_out = refs[6 + len(kv_refs)] if kv else None
        sems = refs[-1]
        at = pl.program_id(0)

        @pl.when(at == 0)
        def _():
            dots[...] = jnp.zeros_like(dots)
            if kv:
                for which in range(2):
                    codes, scales = kv_refs[2 * which], kv_refs[2 * which + 1]
                    factor = scales[...].astype(jnp.float32)
                    for h in range(heads):
                        part = codes[:, :, h * HD : (h + 1) * HD].astype(jnp.float32)
                        rows = part * factor[:, :, h : h + 1]
                        kv_out[h, which * blocks : (which + 1) * blocks] = rows.astype(jnp.bfloat16)

        for h in range(heads):
            pltpu.make_async_copy(
                q_ref.at[:, :, pl.ds(h * HD, HD)], out_ref.at[h, pl.ds(at * step, step)], sems.at[0]
            ).start()
            pltpu.make_async_copy(
                g_ref.at[:, :, pl.ds(h * HD, HD)],
                out_ref.at[h, pl.ds(count + at * step, step)],
                sems.at[1],
            ).start()
        lane = lax.broadcasted_iota(jnp.int32, (step * toks, HD), 1)
        place = lax.broadcasted_iota(jnp.int32, (step * toks, HD), 0) // toks + at * step
        chosen = lane == place
        for h in range(heads):
            cut = slice(h * HD, (h + 1) * HD)
            product = g_ref[:, :, cut].astype(jnp.float32) * f_ref[:, :, cut].astype(jnp.float32)
            total = jnp.sum(product.reshape(step * toks, HD), axis=-1, keepdims=True)
            rows_of = jnp.where(chosen, total, 0.0)
            dots[h] += jnp.sum(rows_of.reshape(step, toks, HD), axis=0)

        @pl.when(at == steps - 1)
        def _():
            for h in range(heads):
                value = dots[h]
                high = value.astype(jnp.bfloat16).astype(jnp.float32)
                middle = (value - high).astype(jnp.bfloat16).astype(jnp.float32)
                low = (value - high - middle).astype(jnp.bfloat16).astype(jnp.float32)
                spread = high + pltpu.roll(middle, PIECE, 1) + pltpu.roll(low, 2 * PIECE, 1)
                dots_out[h, 0] = spread.astype(jnp.bfloat16)
            copies = [
                pltpu.make_async_copy(dots_out, out_ref.at[:, pl.ds(2 * count, 1)], sems.at[2])
            ]
            if kv:
                copies.append(
                    pltpu.make_async_copy(
                        kv_out, out_ref.at[:, pl.ds(2 * count + 1, 2 * blocks)], sems.at[3]
                    )
                )
            for copy in copies:
                copy.start()
            for copy in copies:
                copy.wait()

        pltpu.make_async_copy(q_ref, q_ref, sems.at[0]).wait()
        pltpu.make_async_copy(g_ref, g_ref, sems.at[1]).wait()

    rows = pl.BlockSpec((step, toks, width), lambda i: (start + i, 0, 0))
    in_specs = [rows] * 3
    args = [query, out_grad, forward_out]
    scratch = [
        pltpu.VMEM((heads, toks, HD), jnp.float32),
        pltpu.VMEM((heads, 1, toks, HD), jnp.bfloat16),
    ]
    if kv:
        in_specs += [pl.BlockSpec(x.shape, lambda i: (0, 0, 0)) for x in kv]
        args += list(kv)
        scratch.append(pltpu.VMEM((heads, 2 * blocks, toks, HD), jnp.bfloat16))
    scratch.append(pltpu.SemaphoreType.DMA((4,)))
    return pl.pallas_call(
        body,
        grid=(steps,),
        in_specs=in_specs,
        out_specs=pl.BlockSpec(memory_space=pl.ANY),
        out_shape=jax.ShapeDtypeStruct((heads, slots, toks, HD), jnp.bfloat16),
        scratch_shapes=scratch,
        compiler_params=params(),
    )(*args)


def nt(a, b):
    return lax.dot_general(a, b, (((1,), (1,)), ((), ())), preferred_element_type=jnp.float32)


def nn(a, b):
    return jnp.dot(a, b, preferred_element_type=jnp.float32)


def attend(pairs, message, kv_own, kv_other, first, count, sums=None, extra=0):
    srcs, _, toks, _ = message.shape
    length = srcs * toks
    blocks = kv_own.shape[1] // 2
    total = 2 * blocks
    last = sums is not None

    def body(pair_ref, m_ref, own_ref, other_ref, *refs):
        if last:
            sum_ref, out_ref, own_sum, other_sum = refs[:4]
            refs, (key_acc, value_acc) = refs[4:-2], refs[-2:]
        else:
            out_ref, sum_out = refs[:2]
            refs = refs[2:]
            key_acc, value_acc = sum_out.at[0], sum_out.at[1]
        keys, keys_t, values, dots = refs[:4]
        scores, prob_grads, probs, score_grads, queries, grads = (
            refs[4 + SLOTS * at : 4 + SLOTS * (at + 1)] for at in range(6)
        )
        for b in range(total):
            source, at = (own_ref, b) if b < blocks else (other_ref, b - blocks)
            key = source[:, at].reshape(length, HD)
            keys[b] = key
            keys_t[b] = key.astype(jnp.float32).T.astype(jnp.bfloat16)
            values[b] = source[:, blocks + at].reshape(length, HD)
        row = lax.broadcasted_iota(jnp.int32, (PIECE, HD), 0)
        lane = lax.broadcasted_iota(jnp.int32, (PIECE, HD), 1)
        picks = jnp.where((lane % PIECE == row) & (lane < 3 * PIECE), 1.0, 0.0).astype(jnp.bfloat16)
        dots[...] = nt(picks, m_ref[:, 2 * count].reshape(length, HD))
        if last:
            key_acc[...] = sum_ref[0]
            value_acc[...] = sum_ref[1]
        else:
            sum_out[...] = jnp.zeros_like(sum_out)

        def place(c, j):
            return pair_ref[2 * (first + c) + j]

        def scores_of(c, slot):
            query = m_ref[:, c].reshape(length, HD)
            grad = m_ref[:, count + c].reshape(length, HD)
            queries[slot][...] = query
            grads[slot][...] = grad
            for j in range(2):
                scores[slot][j] = nt(keys[place(c, j)], query)
                prob_grads[slot][j] = nt(values[place(c, j)], grad)

        def probs_of(c, slot):
            score, prob_grad = scores[slot], prob_grads[slot]
            cuts = [(j, slice(r, r + 32)) for j in range(2) for r in range(0, length, 32)]
            high = None
            for j, rows in cuts:
                part = jnp.max(score[j, rows].reshape(32 // 8, 8, length), axis=0)
                high = part if high is None else jnp.maximum(high, part)
            high = jnp.max(high, axis=0, keepdims=True) * EXP_SCALE
            norm = None
            for j, rows in cuts:
                weight = jnp.exp2(score[j, rows] * EXP_SCALE - high)
                score[j, rows] = weight
                part = jnp.sum(weight.reshape(32 // 8, 8, length), axis=0)
                norm = part if norm is None else norm + part
            inverse = 1.0 / jnp.sum(norm, axis=0, keepdims=True)
            dot_row = dots[pl.ds(c, 1), :]
            for j, rows in cuts:
                prob = score[j, rows] * inverse
                probs[slot][j, rows] = prob.astype(jnp.bfloat16)
                score_grads[slot][j, rows] = (prob * (prob_grad[j, rows] - dot_row)).astype(
                    jnp.bfloat16
                )

        def grads_of(c, slot):
            query_t = None
            for j in range(2):
                b = place(c, j)
                value_acc[b] += nn(probs[slot][j], grads[slot][...])
                key_acc[b] += nn(score_grads[slot][j], queries[slot][...])
                part = nn(keys_t[b], score_grads[slot][j])
                query_t = part if query_t is None else query_t + part
            out_ref[:, c] = (query_t * SCALE).T.astype(jnp.bfloat16).reshape(srcs, toks, HD)

        for ref in (probs[-1], score_grads[-1], queries[-1], grads[-1]):
            ref[...] = jnp.zeros_like(ref)
        scores_of(0, 0)

        def several(i, _):
            for k in range(SLOTS):
                c = i * SLOTS + k
                grads_of(jnp.maximum(c - 1, 0), (k - 1) % SLOTS)
                scores_of(jnp.minimum(c + 1, count - 1), (k + 1) % SLOTS)
                probs_of(c, k)
            return 0

        lax.fori_loop(0, count // SLOTS, several, 0)
        grads_of(count - 1, SLOTS - 1)
        if last:
            own_sum[0] = key_acc[:blocks] * SCALE
            own_sum[1] = value_acc[:blocks]
            other_sum[0] = (key_acc[blocks:] * SCALE).astype(jnp.bfloat16)
            other_sum[1] = value_acc[blocks:].astype(jnp.bfloat16)

    def whole(shape):
        return pl.BlockSpec(shape, lambda i, p: (0,) * len(shape))

    dq = jax.ShapeDtypeStruct((srcs, count + extra, toks, HD), jnp.bfloat16)
    dq_spec = whole((srcs, count, toks, HD))
    acc = (2, total, length, HD)
    scratch = [
        pltpu.VMEM((total, length, HD), jnp.bfloat16),
        pltpu.VMEM((total, HD, length), jnp.bfloat16),
        pltpu.VMEM((total, length, HD), jnp.bfloat16),
        pltpu.VMEM((PIECE, length), jnp.float32),
    ]
    scratch += [pltpu.VMEM((2, length, length), jnp.float32)] * (2 * SLOTS)
    scratch += [pltpu.VMEM((2, length, length), jnp.bfloat16)] * (2 * SLOTS)
    scratch += [pltpu.VMEM((length, HD), jnp.bfloat16)] * (2 * SLOTS)
    in_specs = [HELD if last else whole(message.shape), HELD, HELD]
    args = [held(message) if last else message, held(kv_own), held(kv_other)]
    if last:
        part = (2, blocks, length, HD)
        out_shape = (dq, pltpu.VMEM(part, jnp.float32), pltpu.VMEM(part, jnp.bfloat16))
        out_specs = [dq_spec, HELD, HELD]
        scratch += [pltpu.VMEM((total, length, HD), jnp.float32)] * 2
        in_specs.append(HELD)
        args.append(held(sums))
    else:
        out_shape = (dq, pltpu.VMEM(acc, jnp.float32))
        out_specs = [dq_spec, HELD]
    flops = 2 * 5 * count * length * 2 * length * HD
    return pl.pallas_call(
        body,
        grid_spec=pltpu.PrefetchScalarGridSpec(
            num_scalar_prefetch=1,
            grid=(1,),
            in_specs=in_specs,
            out_specs=out_specs,
            scratch_shapes=scratch,
        ),
        out_shape=out_shape,
        compiler_params=params(),
        cost_estimate=pl.CostEstimate(
            flops=flops, transcendentals=2 * count * length * length, bytes_accessed=6 << 20
        ),
    )(pairs, *args)


def combine(message, own_sum, other_sum, count):
    srcs, _, toks, _ = message.shape
    blocks = own_sum.shape[1]

    def body(_, own_ref, other_ref, out_ref):
        which = pl.program_id(0)
        for b in range(blocks):
            value = own_ref[which, b] + other_ref[which, b].astype(jnp.float32)
            out_ref[:, b] = value.astype(jnp.bfloat16).reshape(srcs, toks, HD)

    return pl.pallas_call(
        body,
        name="combine",
        grid=(2,),
        in_specs=[pl.BlockSpec(memory_space=pl.ANY), HELD, HELD],
        out_specs=pl.BlockSpec((srcs, blocks, toks, HD), lambda i: (0, count // blocks + i, 0, 0)),
        out_shape=jax.ShapeDtypeStruct(message.shape, message.dtype),
        input_output_aliases={0: 0},
        compiler_params=params(),
    )(message, held(own_sum), held(other_sum))


def unpack(message, total, first, count, step, into=None, blocks=0):
    heads, _, toks, _ = message.shape
    width = heads * HD
    start = first // step

    def body(m_ref, *refs):
        out_ref, *sums = refs if into is None else refs[1:]
        at = pl.program_id(0) * step
        for h in range(heads):
            out_ref[:, :, h * HD : (h + 1) * HD] = m_ref[h, pl.ds(at, step)]
        for which, out in enumerate(sums):
            behind = count + which * blocks
            for h in range(heads):
                out[:, :, h * HD : (h + 1) * HD] = m_ref[h, behind : behind + blocks]

    in_specs = [HELD]
    args = [held(message)]
    out_shape = [jax.ShapeDtypeStruct((total, toks, width), message.dtype)]
    out_specs = [pl.BlockSpec((step, toks, width), lambda i: (start + i, 0, 0))]
    if blocks:
        out_shape += [jax.ShapeDtypeStruct((blocks, toks, width), message.dtype)] * 2
        out_specs += [pl.BlockSpec((blocks, toks, width), lambda i: (0, 0, 0))] * 2
    aliases = {}
    if into is not None:
        in_specs.append(pl.BlockSpec(memory_space=pl.ANY))
        args.append(into)
        aliases = {1: 0}
    return pl.pallas_call(
        body,
        grid=(count // step,),
        in_specs=in_specs,
        out_specs=out_specs,
        out_shape=out_shape,
        input_output_aliases=aliases,
        compiler_params=params(),
    )(*args)


def to_heads(message):
    return lax.all_to_all(message, "head", split_axis=0, concat_axis=0, tiled=True)


def on_device(
    query, out_grad, forward_out, key_codes, key_scale, value_codes, value_scale, pairing
):
    count = query.shape[0]
    blocks = key_codes.shape[0]
    large = count * 2 // 3
    small = count - large
    swap = [(0, 1), (1, 0)]
    group = lax.axis_index("grp")
    mine = lax.dynamic_slice_in_dim(pairing, group * count, count, 0)
    pairs = ((mine + blocks * group) % (2 * blocks)).reshape(-1)
    codes = (key_codes, key_scale, value_codes, value_scale)
    send0 = pack(query, out_grad, forward_out, 0, large, large, codes)
    got0 = to_heads(send0)
    later, pairs = lax.optimization_barrier((forward_out, pairs))
    send1 = pack(query, out_grad, later, large, small, small)
    got1 = to_heads(send1)
    kv_own = got0[:, 2 * large + 1 :]
    kv_other = lax.ppermute(kv_own, "grp", swap)
    grads0, sums = attend(pairs, got0, kv_own, kv_other, 0, large)
    back0 = to_heads(grads0)
    grads1, own_sum, other_sum = attend(
        pairs, got1, kv_own, kv_other, large, small, sums, extra=2 * blocks
    )
    theirs = lax.ppermute(other_sum, "grp", swap)
    grads1 = combine(grads1, own_sum, theirs, small)
    back1 = to_heads(grads1)
    (rows,) = unpack(back0, count, 0, large, 6)
    return unpack(back1, count, large, small, small, into=rows, blocks=blocks)


def solution(mesh):
    spec = P("grp", "head", None)
    return jax.shard_map(
        on_device,
        mesh=mesh,
        in_specs=(spec,) * 7 + (P(),),
        out_specs=(spec,) * 3,
        check_vma=False,
    )
```

```python
import jax
import jax.numpy as jnp
from jax import lax
from jax.experimental import pallas as pl
from jax.experimental.pallas import tpu as pltpu
from jax.sharding import PartitionSpec as P


HD = 128
SCALE = HD ** (-0.5)
LOG2E = 1.4426950408889634
EXP_SCALE = SCALE * LOG2E
SLOTS = 3
PIECE = 32


HELD = pl.BlockSpec(memory_space=pltpu.VMEM)


def held(x):
    return pltpu.with_memory_space_constraint(x, pltpu.VMEM)


def params(mib=56):
    return pltpu.CompilerParams(vmem_limit_bytes=mib << 20)


def pack(query, out_grad, forward_out, first, count, parts, kv=None):
    _, toks, width = query.shape
    heads = width // HD
    blocks = kv[0].shape[0] if kv else 0
    slots = 2 * count + 1 + 2 * blocks
    step = count // parts

    def body(*refs):
        sources = refs[:3]
        kv_refs = refs[3 : 3 + (4 if kv else 0)]
        out_ref = refs[3 + len(kv_refs)]
        *refs, in_sems, out_sems = refs[4 + len(kv_refs) :]
        q_buf, g_buf, f_buf, dots, dots_out = refs[:5]
        kv_out = refs[5] if kv else None

        def read(which, part):
            buf = (q_buf, g_buf, f_buf)[which]
            return pltpu.make_async_copy(
                sources[which].at[pl.ds(first + part * step, step)],
                buf.at[pl.ds(part * step, step)],
                in_sems.at[which, part],
            )

        def write(which, part, h):
            buf = (q_buf, g_buf)[which]
            pltpu.make_async_copy(
                buf.at[pl.ds(part * step, step), :, pl.ds(h * HD, HD)],
                out_ref.at[h, pl.ds(which * count + part * step, step)],
                out_sems.at[which],
            ).start()

        for part in range(parts):
            for which in (1, 2, 0):
                read(which, part).start()
        if kv:
            for which in range(2):
                codes, scales = kv_refs[2 * which], kv_refs[2 * which + 1]
                factor = scales[...].astype(jnp.float32)
                for h in range(heads):
                    rows = codes[:, :, h * HD : (h + 1) * HD].astype(jnp.float32)
                    rows = rows * factor[:, :, h : h + 1]
                    kv_out[h, which * blocks : (which + 1) * blocks] = rows.astype(jnp.bfloat16)
            kv_copy = pltpu.make_async_copy(
                kv_out, out_ref.at[:, pl.ds(2 * count + 1, 2 * blocks)], out_sems.at[3]
            )
            kv_copy.start()
        lane = lax.broadcasted_iota(jnp.int32, (step * toks, HD), 1)
        place = lax.broadcasted_iota(jnp.int32, (step * toks, HD), 0) // toks
        for part in range(parts):
            rows_at = slice(part * step, (part + 1) * step)
            chosen = lane == place + part * step
            read(1, part).wait()
            read(2, part).wait()
            for h in range(heads):
                write(1, part, h)
            read(0, part).wait()
            for h in range(heads):
                write(0, part, h)
            for h in range(heads):
                cut = slice(h * HD, (h + 1) * HD)
                product = g_buf[rows_at, :, cut].astype(jnp.float32)
                product *= f_buf[rows_at, :, cut].astype(jnp.float32)
                total = jnp.sum(product.reshape(step * toks, HD), axis=-1, keepdims=True)
                rows = jnp.where(chosen, total, 0.0).reshape(step, toks, HD)
                value = jnp.sum(rows, axis=0)
                dots[h] = value if part == 0 else dots[h] + value
        for h in range(heads):
            value = dots[h]
            high = value.astype(jnp.bfloat16).astype(jnp.float32)
            middle = (value - high).astype(jnp.bfloat16).astype(jnp.float32)
            low = (value - high - middle).astype(jnp.bfloat16).astype(jnp.float32)
            spread = high + pltpu.roll(middle, PIECE, 1) + pltpu.roll(low, 2 * PIECE, 1)
            dots_out[h, 0] = spread.astype(jnp.bfloat16)
        dots_copy = pltpu.make_async_copy(
            dots_out, out_ref.at[:, pl.ds(2 * count, 1)], out_sems.at[2]
        )
        dots_copy.start()
        if kv:
            kv_copy.wait()
        pltpu.make_async_copy(g_buf, g_buf, out_sems.at[1]).wait()
        pltpu.make_async_copy(q_buf, q_buf, out_sems.at[0]).wait()
        dots_copy.wait()

    in_specs = [pl.BlockSpec(memory_space=pl.ANY)] * 3
    args = [query, out_grad, forward_out]
    scratch = [pltpu.VMEM((count, toks, width), jnp.bfloat16)] * 3
    scratch.append(pltpu.VMEM((heads, toks, HD), jnp.float32))
    scratch.append(pltpu.VMEM((heads, 1, toks, HD), jnp.bfloat16))
    if kv:
        in_specs += [pl.BlockSpec(x.shape, lambda i: (0, 0, 0)) for x in kv]
        args += list(kv)
        scratch.append(pltpu.VMEM((heads, 2 * blocks, toks, HD), jnp.bfloat16))
    scratch += [pltpu.SemaphoreType.DMA((3, parts)), pltpu.SemaphoreType.DMA((4,))]
    return pl.pallas_call(
        body,
        grid=(1,),
        in_specs=in_specs,
        out_specs=pl.BlockSpec(memory_space=pl.ANY),
        out_shape=jax.ShapeDtypeStruct((heads, slots, toks, HD), jnp.bfloat16),
        scratch_shapes=scratch,
        compiler_params=params(),
    )(*args)


def nt(a, b):
    return lax.dot_general(a, b, (((1,), (1,)), ((), ())), preferred_element_type=jnp.float32)


def nn(a, b):
    return jnp.dot(a, b, preferred_element_type=jnp.float32)


def attend(pairs, message, kv_own, kv_other, first, count, sums=None, extra=0):
    srcs, _, toks, _ = message.shape
    length = srcs * toks
    blocks = kv_own.shape[1] // 2
    total = 2 * blocks
    last = sums is not None

    def body(pair_ref, m_ref, own_ref, other_ref, *refs):
        if last:
            sum_ref, out_ref, own_sum, other_sum = refs[:4]
            refs, (key_acc, value_acc) = refs[4:-2], refs[-2:]
        else:
            out_ref, sum_out = refs[:2]
            refs = refs[2:]
            key_acc, value_acc = sum_out.at[0], sum_out.at[1]
        keys, keys_t, values, dots = refs[:4]
        scores, prob_grads, probs, score_grads, queries, grads = (
            refs[4 + SLOTS * at : 4 + SLOTS * (at + 1)] for at in range(6)
        )
        for b in range(total):
            source, at = (own_ref, b) if b < blocks else (other_ref, b - blocks)
            key = source[:, at].reshape(length, HD)
            keys[b] = key
            keys_t[b] = key.astype(jnp.float32).T.astype(jnp.bfloat16)
            values[b] = source[:, blocks + at].reshape(length, HD)
        row = lax.broadcasted_iota(jnp.int32, (PIECE, HD), 0)
        lane = lax.broadcasted_iota(jnp.int32, (PIECE, HD), 1)
        picks = jnp.where((lane % PIECE == row) & (lane < 3 * PIECE), 1.0, 0.0).astype(jnp.bfloat16)
        dots[...] = nt(picks, m_ref[:, 2 * count].reshape(length, HD))
        if last:
            key_acc[...] = sum_ref[0]
            value_acc[...] = sum_ref[1]
        else:
            sum_out[...] = jnp.zeros_like(sum_out)

        def place(c, j):
            return pair_ref[2 * (first + c) + j]

        def scores_of(c, slot):
            query = m_ref[:, c].reshape(length, HD)
            grad = m_ref[:, count + c].reshape(length, HD)
            queries[slot][...] = query
            grads[slot][...] = grad
            for j in range(2):
                scores[slot][j] = nt(keys[place(c, j)], query)
                prob_grads[slot][j] = nt(values[place(c, j)], grad)

        def probs_of(c, slot):
            score, prob_grad = scores[slot], prob_grads[slot]
            cuts = [(j, slice(r, r + 32)) for j in range(2) for r in range(0, length, 32)]
            high = None
            for j, rows in cuts:
                part = jnp.max(score[j, rows].reshape(32 // 8, 8, length), axis=0)
                high = part if high is None else jnp.maximum(high, part)
            high = jnp.max(high, axis=0, keepdims=True) * EXP_SCALE
            norm = None
            for j, rows in cuts:
                weight = jnp.exp2(score[j, rows] * EXP_SCALE - high)
                score[j, rows] = weight
                part = jnp.sum(weight.reshape(32 // 8, 8, length), axis=0)
                norm = part if norm is None else norm + part
            inverse = 1.0 / jnp.sum(norm, axis=0, keepdims=True)
            dot_row = dots[pl.ds(c, 1), :]
            for j, rows in cuts:
                prob = score[j, rows] * inverse
                probs[slot][j, rows] = prob.astype(jnp.bfloat16)
                score_grads[slot][j, rows] = (prob * (prob_grad[j, rows] - dot_row)).astype(
                    jnp.bfloat16
                )

        def grads_of(c, slot):
            value_part = nn(probs[slot][...].reshape(2 * length, length), grads[slot][...])
            key_part = nn(score_grads[slot][...].reshape(2 * length, length), queries[slot][...])
            query_t = None
            for j in range(2):
                b = place(c, j)
                rows = slice(j * length, (j + 1) * length)
                value_acc[b] += value_part[rows]
                key_acc[b] += key_part[rows]
                part = nn(keys_t[b], score_grads[slot][j])
                query_t = part if query_t is None else query_t + part
            out_ref[:, c] = (query_t * SCALE).T.astype(jnp.bfloat16).reshape(srcs, toks, HD)

        for ref in (probs[-1], score_grads[-1], queries[-1], grads[-1]):
            ref[...] = jnp.zeros_like(ref)
        scores_of(0, 0)

        def several(i, _):
            for k in range(SLOTS):
                c = i * SLOTS + k
                grads_of(jnp.maximum(c - 1, 0), (k - 1) % SLOTS)
                scores_of(jnp.minimum(c + 1, count - 1), (k + 1) % SLOTS)
                probs_of(c, k)
            return 0

        lax.fori_loop(0, count // SLOTS, several, 0)
        grads_of(count - 1, SLOTS - 1)
        if last:
            own_sum[0] = key_acc[:blocks] * SCALE
            own_sum[1] = value_acc[:blocks]
            other_sum[0] = (key_acc[blocks:] * SCALE).astype(jnp.bfloat16)
            other_sum[1] = value_acc[blocks:].astype(jnp.bfloat16)

    def whole(shape):
        return pl.BlockSpec(shape, lambda i, p: (0,) * len(shape))

    dq = jax.ShapeDtypeStruct((srcs, count + extra, toks, HD), jnp.bfloat16)
    dq_spec = whole((srcs, count, toks, HD))
    acc = (2, total, length, HD)
    scratch = [
        pltpu.VMEM((total, length, HD), jnp.bfloat16),
        pltpu.VMEM((total, HD, length), jnp.bfloat16),
        pltpu.VMEM((total, length, HD), jnp.bfloat16),
        pltpu.VMEM((PIECE, length), jnp.float32),
    ]
    scratch += [pltpu.VMEM((2, length, length), jnp.float32)] * (2 * SLOTS)
    scratch += [pltpu.VMEM((2, length, length), jnp.bfloat16)] * (2 * SLOTS)
    scratch += [pltpu.VMEM((length, HD), jnp.bfloat16)] * (2 * SLOTS)
    in_specs = [whole(x.shape) for x in (message, kv_own, kv_other)]
    args = [message, kv_own, kv_other]
    if last:
        in_specs[0], args[0] = HELD, held(message)
    if last:
        part = (2, blocks, length, HD)
        out_shape = (dq, pltpu.VMEM(part, jnp.float32), pltpu.VMEM(part, jnp.bfloat16))
        out_specs = [dq_spec, HELD, HELD]
        scratch += [pltpu.VMEM((total, length, HD), jnp.float32)] * 2
        in_specs.append(whole(acc))
        args.append(sums)
    else:
        out_shape = (dq, jax.ShapeDtypeStruct(acc, jnp.float32))
        out_specs = [dq_spec, whole(acc)]
    flops = 2 * 5 * count * length * 2 * length * HD
    return pl.pallas_call(
        body,
        grid_spec=pltpu.PrefetchScalarGridSpec(
            num_scalar_prefetch=1,
            grid=(1,),
            in_specs=in_specs,
            out_specs=out_specs,
            scratch_shapes=scratch,
        ),
        out_shape=out_shape,
        compiler_params=params(),
        cost_estimate=pl.CostEstimate(
            flops=flops, transcendentals=2 * count * length * length, bytes_accessed=6 << 20
        ),
    )(pairs, *args)


def combine(message, own_sum, other_sum, count):
    srcs, _, toks, _ = message.shape
    blocks = own_sum.shape[1]

    def body(_, own_ref, other_ref, out_ref):
        which = pl.program_id(0)
        for b in range(blocks):
            value = own_ref[which, b] + other_ref[which, b].astype(jnp.float32)
            out_ref[:, b] = value.astype(jnp.bfloat16).reshape(srcs, toks, HD)

    return pl.pallas_call(
        body,
        name="combine",
        grid=(2,),
        in_specs=[pl.BlockSpec(memory_space=pl.ANY), HELD, HELD],
        out_specs=pl.BlockSpec((srcs, blocks, toks, HD), lambda i: (0, count // blocks + i, 0, 0)),
        out_shape=jax.ShapeDtypeStruct(message.shape, message.dtype),
        input_output_aliases={0: 0},
        compiler_params=params(),
    )(message, held(own_sum), held(other_sum))


def unpack(message, total, first, count, step, into=None, blocks=0):
    heads, _, toks, _ = message.shape
    width = heads * HD
    start = first // step

    def body(m_ref, *refs):
        out_ref, *sums = refs if into is None else refs[1:]
        at = pl.program_id(0) * step
        for h in range(heads):
            out_ref[:, :, h * HD : (h + 1) * HD] = m_ref[h, pl.ds(at, step)]
        for which, out in enumerate(sums):
            behind = count + which * blocks
            for h in range(heads):
                out[:, :, h * HD : (h + 1) * HD] = m_ref[h, behind : behind + blocks]

    in_specs = [HELD]
    args = [held(message)]
    out_shape = [jax.ShapeDtypeStruct((total, toks, width), message.dtype)]
    out_specs = [pl.BlockSpec((step, toks, width), lambda i: (start + i, 0, 0))]
    if blocks:
        out_shape += [jax.ShapeDtypeStruct((blocks, toks, width), message.dtype)] * 2
        out_specs += [pl.BlockSpec((blocks, toks, width), lambda i: (0, 0, 0))] * 2
    aliases = {}
    if into is not None:
        in_specs.append(pl.BlockSpec(memory_space=pl.ANY))
        args.append(into)
        aliases = {1: 0}
    return pl.pallas_call(
        body,
        grid=(count // step,),
        in_specs=in_specs,
        out_specs=out_specs,
        out_shape=out_shape,
        input_output_aliases=aliases,
        compiler_params=params(),
    )(*args)


def to_heads(message):
    return lax.all_to_all(message, "head", split_axis=0, concat_axis=0, tiled=True)


def on_device(
    query, out_grad, forward_out, key_codes, key_scale, value_codes, value_scale, pairing
):
    count = query.shape[0]
    blocks = key_codes.shape[0]
    large = count * 2 // 3
    small = count - large
    swap = [(0, 1), (1, 0)]
    group = lax.axis_index("grp")
    mine = lax.dynamic_slice_in_dim(pairing, group * count, count, 0)
    pairs = ((mine + blocks * group) % (2 * blocks)).reshape(-1)
    codes = (key_codes, key_scale, value_codes, value_scale)
    send0 = pack(query, out_grad, forward_out, 0, large, 2, codes)
    got0 = to_heads(send0)
    later, pairs = lax.optimization_barrier((forward_out, pairs))
    send1 = pack(query, out_grad, later, large, small, 1)
    got1 = to_heads(send1)
    kv_own = got0[:, 2 * large + 1 :]
    kv_other = lax.ppermute(kv_own, "grp", swap)
    grads0, sums = attend(pairs, got0, kv_own, kv_other, 0, large)
    back0 = to_heads(grads0)
    grads1, own_sum, other_sum = attend(
        pairs, got1, kv_own, kv_other, large, small, sums, extra=2 * blocks
    )
    theirs = lax.ppermute(other_sum, "grp", swap)
    grads1 = combine(grads1, own_sum, theirs, small)
    back1 = to_heads(grads1)
    (rows,) = unpack(back0, count, 0, large, 6)
    return unpack(back1, count, large, small, small, into=rows, blocks=blocks)


def solution(mesh):
    spec = P("grp", "head", None)
    return jax.shard_map(
        on_device,
        mesh=mesh,
        in_specs=(spec,) * 7 + (P(),),
        out_specs=(spec,) * 3,
        check_vma=False,
    )
```

```python
import jax
import jax.numpy as jnp
from jax import lax
from jax.experimental import pallas as pl
from jax.experimental.pallas import tpu as pltpu
from jax.sharding import PartitionSpec as P

HD = 128
SCALE = HD ** (-0.5)
LOG2E = 1.4426950408889634
EXP_SCALE = SCALE * LOG2E
SLOTS = 3
PIECE = 32


HELD = pl.BlockSpec(memory_space=pltpu.VMEM)


def held(x):
    return pltpu.with_memory_space_constraint(x, pltpu.VMEM)


def params(mib=56):
    return pltpu.CompilerParams(vmem_limit_bytes=mib << 20)


def pack(query, out_grad, forward_out, first, count, parts, kv=None):
    _, toks, width = query.shape
    heads = width // HD
    blocks = kv[0].shape[0] if kv else 0
    step = count // parts
    ahead = 2 * blocks
    slots = ahead + 2 * step + 1

    def body(*refs):
        sources = refs[:3]
        kv_refs = refs[3 : 3 + (4 if kv else 0)]
        out_ref = refs[3 + len(kv_refs)]
        *refs, in_sems, out_sems = refs[4 + len(kv_refs) :]
        q_buf, g_buf, f_buf, dots, dots_out = refs[:5]
        kv_out = refs[5] if kv else None

        def read(which, part):
            buf = (q_buf, g_buf, f_buf)[which]
            return pltpu.make_async_copy(
                sources[which].at[pl.ds(first + part * step, step)],
                buf.at[pl.ds(part * step, step)],
                in_sems.at[which, part],
            )

        def write(which, part, h):
            buf = (q_buf, g_buf)[which]
            pltpu.make_async_copy(
                buf.at[pl.ds(part * step, step), :, pl.ds(h * HD, HD)],
                out_ref.at[part * heads + h, pl.ds(ahead + which * step, step)],
                out_sems.at[which],
            ).start()

        for part in range(parts):
            for which in (1, 2, 0):
                read(which, part).start()
        if kv:
            for which in range(2):
                codes, scales = kv_refs[2 * which], kv_refs[2 * which + 1]
                factor = scales[...].astype(jnp.float32)
                for h in range(heads):
                    rows = codes[:, :, h * HD : (h + 1) * HD].astype(jnp.float32)
                    rows = rows * factor[:, :, h : h + 1]
                    kv_out[h, which * blocks : (which + 1) * blocks] = rows.astype(jnp.bfloat16)
            kv_copies = [
                pltpu.make_async_copy(
                    kv_out,
                    out_ref.at[pl.ds(part * heads, heads), pl.ds(0, ahead)],
                    out_sems.at[3 + part],
                )
                for part in range(parts)
            ]
            for copy in kv_copies:
                copy.start()
        lane = lax.broadcasted_iota(jnp.int32, (step * toks, HD), 1)
        place = lax.broadcasted_iota(jnp.int32, (step * toks, HD), 0) // toks
        chosen = lane == place
        for part in range(parts):
            rows_at = slice(part * step, (part + 1) * step)
            read(1, part).wait()
            read(2, part).wait()
            for h in range(heads):
                write(1, part, h)
            read(0, part).wait()
            for h in range(heads):
                write(0, part, h)
            for h in range(heads):
                cut = slice(h * HD, (h + 1) * HD)
                product = g_buf[rows_at, :, cut].astype(jnp.float32)
                product *= f_buf[rows_at, :, cut].astype(jnp.float32)
                total = jnp.sum(product.reshape(step * toks, HD), axis=-1, keepdims=True)
                rows = jnp.where(chosen, total, 0.0).reshape(step, toks, HD)
                dots[part * heads + h] = jnp.sum(rows, axis=0)
        for h in range(parts * heads):
            value = dots[h]
            high = value.astype(jnp.bfloat16).astype(jnp.float32)
            middle = (value - high).astype(jnp.bfloat16).astype(jnp.float32)
            low = (value - high - middle).astype(jnp.bfloat16).astype(jnp.float32)
            spread = high + pltpu.roll(middle, PIECE, 1) + pltpu.roll(low, 2 * PIECE, 1)
            dots_out[h, 0] = spread.astype(jnp.bfloat16)
        dots_copy = pltpu.make_async_copy(
            dots_out, out_ref.at[:, pl.ds(ahead + 2 * step, 1)], out_sems.at[2]
        )
        dots_copy.start()
        if kv:
            for copy in kv_copies:
                copy.wait()
        pltpu.make_async_copy(g_buf, g_buf, out_sems.at[1]).wait()
        pltpu.make_async_copy(q_buf, q_buf, out_sems.at[0]).wait()
        dots_copy.wait()

    in_specs = [pl.BlockSpec(memory_space=pl.ANY)] * 3
    args = [query, out_grad, forward_out]
    scratch = [pltpu.VMEM((count, toks, width), jnp.bfloat16)] * 3
    scratch.append(pltpu.VMEM((parts * heads, toks, HD), jnp.float32))
    scratch.append(pltpu.VMEM((parts * heads, 1, toks, HD), jnp.bfloat16))
    if kv:
        in_specs += [pl.BlockSpec(x.shape, lambda i: (0, 0, 0)) for x in kv]
        args += list(kv)
        scratch.append(pltpu.VMEM((heads, 2 * blocks, toks, HD), jnp.bfloat16))
    scratch += [pltpu.SemaphoreType.DMA((3, parts)), pltpu.SemaphoreType.DMA((3 + parts,))]
    return pl.pallas_call(
        body,
        name=f"pack{first}",
        grid=(1,),
        in_specs=in_specs,
        out_specs=pl.BlockSpec(memory_space=pl.ANY),
        out_shape=jax.ShapeDtypeStruct((parts * heads, slots, toks, HD), jnp.bfloat16),
        scratch_shapes=scratch,
        compiler_params=params(),
    )(*args)


def nt(a, b):
    return lax.dot_general(a, b, (((1,), (1,)), ((), ())), preferred_element_type=jnp.float32)


def nn(a, b):
    return jnp.dot(a, b, preferred_element_type=jnp.float32)


def attend(pairs, message, source, first, per, count, groups, blocks, sums=None):
    devices, slots, toks, _ = message.shape
    srcs = devices // groups
    length = srcs * toks
    total = groups * blocks
    steps = groups * count
    last = sums is not None
    ahead = slots - 2 * count - 1
    extra = 2 * blocks if last else 0

    def body(pair_ref, group_ref, m_ref, kv_ref, *refs):
        if last:
            sum_ref, out_ref = refs[:2]
            refs, (key_acc, value_acc) = refs[2:-2], refs[-2:]
        else:
            out_ref, sum_out = refs[:2]
            refs = refs[2:]
            key_acc, value_acc = sum_out.at[0], sum_out.at[1]
        keys, keys_t, values, dots = refs[:4]
        scores, prob_grads, probs, score_grads, queries, grads = (
            refs[4 + SLOTS * at : 4 + SLOTS * (at + 1)] for at in range(6)
        )
        for b in range(total):
            rows, at = slice(b // blocks * srcs, (b // blocks + 1) * srcs), b % blocks
            key = kv_ref[rows, at].reshape(length, HD)
            keys[b] = key
            keys_t[b] = key.astype(jnp.float32).T.astype(jnp.bfloat16)
            values[b] = kv_ref[rows, blocks + at].reshape(length, HD)
        row = lax.broadcasted_iota(jnp.int32, (PIECE, HD), 0)
        lane = lax.broadcasted_iota(jnp.int32, (PIECE, HD), 1)
        picks = jnp.where((lane % PIECE == row) & (lane < 3 * PIECE), 1.0, 0.0).astype(jnp.bfloat16)
        for g in range(groups):
            tile = m_ref[g * srcs : (g + 1) * srcs, ahead + 2 * count].reshape(length, HD)
            dots[g * PIECE : (g + 1) * PIECE] = nt(picks, tile)
        if last:
            key_acc[...] = sum_ref[0]
            value_acc[...] = sum_ref[1]
        else:
            sum_out[...] = jnp.zeros_like(sum_out)

        def where(c):
            group = lax.div(c, jnp.int32(count))
            return group, c - group * count

        def place(c, j):
            group, at = where(c)
            block = group * per + first + group_ref[0] * count + at
            return pair_ref[2 * block + j]

        def scores_of(c, slot):
            group, at = where(c)
            rows = pl.ds(group * srcs, srcs)
            query = m_ref[rows, ahead + at].reshape(length, HD)
            grad = m_ref[rows, ahead + count + at].reshape(length, HD)
            queries[slot][...] = query
            grads[slot][...] = grad
            for j in range(2):
                scores[slot][j] = nt(keys[place(c, j)], query)
                prob_grads[slot][j] = nt(values[place(c, j)], grad)

        def probs_of(c, slot):
            score, prob_grad = scores[slot], prob_grads[slot]
            cuts = [(j, slice(r, r + 32)) for j in range(2) for r in range(0, length, 32)]
            high = None
            for j, rows in cuts:
                part = jnp.max(score[j, rows].reshape(32 // 8, 8, length), axis=0)
                high = part if high is None else jnp.maximum(high, part)
            high = jnp.max(high, axis=0, keepdims=True) * EXP_SCALE
            norm = None
            for j, rows in cuts:
                weight = jnp.exp2(score[j, rows] * EXP_SCALE - high)
                score[j, rows] = weight
                part = jnp.sum(weight.reshape(32 // 8, 8, length), axis=0)
                norm = part if norm is None else norm + part
            inverse = 1.0 / jnp.sum(norm, axis=0, keepdims=True)
            group, at = where(c)
            dot_row = dots[pl.ds(group * PIECE + at, 1), :]
            for j, rows in cuts:
                prob = score[j, rows] * inverse
                probs[slot][j, rows] = prob.astype(jnp.bfloat16)
                score_grads[slot][j, rows] = (prob * (prob_grad[j, rows] - dot_row)).astype(
                    jnp.bfloat16
                )

        def grads_of(c, slot):
            value_part = nn(probs[slot][...].reshape(2 * length, length), grads[slot][...])
            key_part = nn(score_grads[slot][...].reshape(2 * length, length), queries[slot][...])
            query_t = None
            for j in range(2):
                b = place(c, j)
                rows = slice(j * length, (j + 1) * length)
                value_acc[b] += value_part[rows]
                key_acc[b] += key_part[rows]
                part = nn(keys_t[b], score_grads[slot][j])
                query_t = part if query_t is None else query_t + part
            group, at = where(c)
            rows = (query_t * SCALE).T.astype(jnp.bfloat16)
            out_ref[pl.ds(group * srcs, srcs), at] = rows.reshape(srcs, toks, HD)

        for ref in (probs[-1], score_grads[-1], queries[-1], grads[-1]):
            ref[...] = jnp.zeros_like(ref)
        scores_of(jnp.int32(0), 0)

        def several(i, _):
            for k in range(SLOTS):
                c = i * SLOTS + k
                grads_of(jnp.maximum(c - 1, 0), (k - 1) % SLOTS)
                scores_of(jnp.minimum(c + 1, steps - 1), (k + 1) % SLOTS)
                probs_of(c, k)
            return 0

        lax.fori_loop(0, steps // SLOTS, several, 0)
        grads_of(jnp.int32(steps - 1), SLOTS - 1)
        if last:
            for b in range(total):
                rows, at = slice(b // blocks * srcs, (b // blocks + 1) * srcs), count + b % blocks
                key_rows = (key_acc[b] * SCALE).astype(jnp.bfloat16)
                out_ref[rows, at] = key_rows.reshape(srcs, toks, HD)
                value_rows = value_acc[b].astype(jnp.bfloat16)
                out_ref[rows, at + blocks] = value_rows.reshape(srcs, toks, HD)

    def whole(shape):
        return pl.BlockSpec(shape, lambda i, p, g: (0,) * len(shape))

    dq = jax.ShapeDtypeStruct((devices, count + extra, toks, HD), jnp.bfloat16)
    acc = (2, total, length, HD)
    scratch = [
        pltpu.VMEM((total, length, HD), jnp.bfloat16),
        pltpu.VMEM((total, HD, length), jnp.bfloat16),
        pltpu.VMEM((total, length, HD), jnp.bfloat16),
        pltpu.VMEM((groups * PIECE, length), jnp.float32),
    ]
    scratch += [pltpu.VMEM((2, length, length), jnp.float32)] * (2 * SLOTS)
    scratch += [pltpu.VMEM((2, length, length), jnp.bfloat16)] * (2 * SLOTS)
    scratch += [pltpu.VMEM((length, HD), jnp.bfloat16)] * (2 * SLOTS)
    in_specs = [whole(message.shape), whole((devices, 2 * blocks, toks, HD))]
    args = [message, source]
    if last:
        in_specs[0], args[0] = HELD, held(message)
        in_specs.append(whole(acc))
        args.append(sums)
        out_shape, out_specs = dq, whole(dq.shape)
        scratch += [pltpu.VMEM((total, length, HD), jnp.float32)] * 2
    else:
        out_shape = (dq, jax.ShapeDtypeStruct(acc, jnp.float32))
        out_specs = [whole(dq.shape), whole(acc)]
    flops = 2 * 5 * steps * length * 2 * length * HD
    return pl.pallas_call(
        body,
        name=f"attend{first}",
        grid_spec=pltpu.PrefetchScalarGridSpec(
            num_scalar_prefetch=2,
            grid=(1,),
            in_specs=in_specs,
            out_specs=out_specs,
            scratch_shapes=scratch,
        ),
        out_shape=out_shape,
        compiler_params=params(),
        cost_estimate=pl.CostEstimate(
            flops=flops, transcendentals=2 * steps * length * length, bytes_accessed=6 << 20
        ),
    )(*pairs, *args)


def unpack(message, total, first, count, step, groups, into=None, blocks=0):
    devices, _, toks, _ = message.shape
    heads = devices // groups
    width = heads * HD
    start = first // step
    per = count // step

    def body(m_ref, *refs):
        out_ref, *sums = refs if into is None else refs[1:]
        part = lax.div(pl.program_id(0), jnp.int32(per))
        at = (pl.program_id(0) - part * per) * step
        for h in range(heads):
            out_ref[:, :, h * HD : (h + 1) * HD] = m_ref[part * heads + h, pl.ds(at, step)]
        if blocks:

            @pl.when(pl.program_id(0) == 0)
            def _():
                for which, out in enumerate(sums):
                    behind = slice(count + which * blocks, count + (which + 1) * blocks)
                    for h in range(heads):
                        value = m_ref[h, behind].astype(jnp.float32)
                        for g in range(1, groups):
                            value += m_ref[g * heads + h, behind].astype(jnp.float32)
                        out[:, :, h * HD : (h + 1) * HD] = value.astype(jnp.bfloat16)

    in_specs = [HELD]
    args = [held(message)]
    out_shape = [jax.ShapeDtypeStruct((total, toks, width), message.dtype)]
    out_specs = [pl.BlockSpec((step, toks, width), lambda i: (start + i, 0, 0))]
    if blocks:
        out_shape += [jax.ShapeDtypeStruct((blocks, toks, width), message.dtype)] * 2
        out_specs += [pl.BlockSpec((blocks, toks, width), lambda i: (0, 0, 0))] * 2
    aliases = {}
    if into is not None:
        in_specs.append(pl.BlockSpec(memory_space=pl.ANY))
        args.append(into)
        aliases = {1: 0}
    return pl.pallas_call(
        body,
        name=f"unpack{first}",
        grid=(groups * per,),
        in_specs=in_specs,
        out_specs=out_specs,
        out_shape=out_shape,
        input_output_aliases=aliases,
        compiler_params=params(),
    )(*args)


def exchange(message):
    return lax.all_to_all(message, ("grp", "head"), split_axis=0, concat_axis=0, tiled=True)


def on_device(
    query, out_grad, forward_out, key_codes, key_scale, value_codes, value_scale, pairing
):
    per = query.shape[0]
    blocks = key_codes.shape[0]
    groups = lax.axis_size("grp")
    large = per * 2 // 3
    small = per - large
    pairs = pairing.reshape(-1)
    group = lax.axis_index("grp").reshape(1)
    codes = (key_codes, key_scale, value_codes, value_scale)
    got0 = exchange(pack(query, out_grad, forward_out, 0, large, groups, codes))
    later, pairs, group = lax.optimization_barrier((forward_out, pairs, group))
    got1 = exchange(pack(query, out_grad, later, large, small, groups))
    pairs = (pairs, group)
    first, second = large // groups, small // groups
    grads0, sums = attend(pairs, got0, got0, 0, per, first, groups, blocks)
    back0 = exchange(grads0)
    grads1 = attend(pairs, got1, got0, large, per, second, groups, blocks, sums)
    back1 = exchange(grads1)
    (rows,) = unpack(back0, per, 0, first, 6, groups)
    return unpack(back1, per, large, second, 6, groups, into=rows, blocks=blocks)


def solution(mesh):
    spec = P("grp", "head", None)
    return jax.shard_map(
        on_device,
        mesh=mesh,
        in_specs=(spec,) * 7 + (P(),),
        out_specs=(spec,) * 3,
        check_vma=False,
    )
```

```python
import jax
import jax.numpy as jnp
from jax import lax
from jax.experimental import pallas as pl
from jax.experimental.pallas import tpu as pltpu
from jax.sharding import PartitionSpec as P

HD = 128
SCALE = HD ** (-0.5)
LOG2E = 1.4426950408889634
EXP_SCALE = SCALE * LOG2E
SLOTS = 3
PIECE = 32


HELD = pl.BlockSpec(memory_space=pltpu.VMEM)


def held(x):
    return pltpu.with_memory_space_constraint(x, pltpu.VMEM)


def params(mib=56):
    return pltpu.CompilerParams(vmem_limit_bytes=mib << 20)


def pack(query, out_grad, first, count, parts, forward_out=None, kv=()):
    total, toks, width = query.shape
    heads = width // HD
    ahead = 2 * kv[0].shape[0] if kv else 0
    blocks = ahead // 2
    step = count // parts
    rest = (total - first - count) // parts
    slots = ahead + 2 * step + (1 if kv else 0)

    def body(*refs):
        sources = refs[: 3 if kv else 2]
        kv_refs = refs[len(sources) : len(sources) + len(kv)]
        out_ref = refs[len(sources) + len(kv)]
        *refs, in_sems, out_sems = refs[len(sources) + len(kv) + 1 :]
        bufs = refs[: len(sources)]
        if kv:
            more, (dots, dots_out, kv_out) = refs[3:5], refs[5:]

        def read(which, part):
            return pltpu.make_async_copy(
                sources[which].at[pl.ds(first + part * step, step)],
                bufs[which].at[pl.ds(part * step, step)],
                in_sems.at[which, part],
            )

        def read_more(which):
            return pltpu.make_async_copy(
                sources[which].at[pl.ds(first + count, rest * parts)],
                more[which - 1],
                in_sems.at[2 + which, 0],
            )

        def write(which, part, h):
            pltpu.make_async_copy(
                bufs[which].at[pl.ds(part * step, step), :, pl.ds(h * HD, HD)],
                out_ref.at[part * heads + h, pl.ds(ahead + which * step, step)],
                out_sems.at[which],
            ).start()

        def row_dots(part, grad, other, rows, size, offset):
            lane = lax.broadcasted_iota(jnp.int32, (size * toks, HD), 1)
            chosen = lane == lax.broadcasted_iota(jnp.int32, (size * toks, HD), 0) // toks + offset
            for h in range(heads):
                cut = slice(h * HD, (h + 1) * HD)
                product = grad[rows, :, cut].astype(jnp.float32)
                product *= other[rows, :, cut].astype(jnp.float32)
                sums = jnp.sum(product.reshape(size * toks, HD), axis=-1, keepdims=True)
                value = jnp.sum(jnp.where(chosen, sums, 0.0).reshape(size, toks, HD), axis=0)
                at = part * heads + h
                dots[at] = value if offset == 0 else dots[at] + value

        for part in range(parts):
            for which in (1, 2, 0) if kv else (1, 0):
                read(which, part).start()
        if kv:
            read_more(1).start()
            read_more(2).start()
            for which in range(2):
                codes, scales = kv_refs[2 * which], kv_refs[2 * which + 1]
                factor = scales[...].astype(jnp.float32)
                for h in range(heads):
                    rows = codes[:, :, h * HD : (h + 1) * HD].astype(jnp.float32)
                    rows = rows * factor[:, :, h : h + 1]
                    kv_out[h, which * blocks : (which + 1) * blocks] = rows.astype(jnp.bfloat16)
            kv_copies = [
                pltpu.make_async_copy(
                    kv_out,
                    out_ref.at[pl.ds(part * heads, heads), pl.ds(0, ahead)],
                    out_sems.at[3 + part],
                )
                for part in range(parts)
            ]
            for copy in kv_copies:
                copy.start()
        for part in range(parts):
            for which in (1, 2, 0) if kv else (1, 0):
                read(which, part).wait()
            for which in (1, 0):
                for h in range(heads):
                    write(which, part, h)
            if kv:
                row_dots(part, bufs[1], bufs[2], slice(part * step, (part + 1) * step), step, 0)
        if kv:
            read_more(1).wait()
            read_more(2).wait()
            for part in range(parts):
                row_dots(part, *more, slice(part * rest, (part + 1) * rest), rest, step)
            for h in range(parts * heads):
                value = dots[h]
                high = value.astype(jnp.bfloat16).astype(jnp.float32)
                middle = (value - high).astype(jnp.bfloat16).astype(jnp.float32)
                low = (value - high - middle).astype(jnp.bfloat16).astype(jnp.float32)
                spread = high + pltpu.roll(middle, PIECE, 1) + pltpu.roll(low, 2 * PIECE, 1)
                dots_out[h, 0] = spread.astype(jnp.bfloat16)
            dots_copy = pltpu.make_async_copy(
                dots_out, out_ref.at[:, pl.ds(ahead + 2 * step, 1)], out_sems.at[2]
            )
            dots_copy.start()
            for copy in kv_copies:
                copy.wait()
        for which in (1, 0):
            pltpu.make_async_copy(bufs[which], bufs[which], out_sems.at[which]).wait()
        if kv:
            dots_copy.wait()

    args = [query, out_grad] + ([forward_out] if kv else [])
    in_specs = [pl.BlockSpec(memory_space=pl.ANY)] * len(args)
    scratch = [pltpu.VMEM((count, toks, width), jnp.bfloat16)] * len(args)
    if kv:
        in_specs += [pl.BlockSpec(x.shape, lambda i: (0, 0, 0)) for x in kv]
        args += list(kv)
        scratch += [pltpu.VMEM((rest * parts, toks, width), jnp.bfloat16)] * 2
        scratch.append(pltpu.VMEM((parts * heads, toks, HD), jnp.float32))
        scratch.append(pltpu.VMEM((parts * heads, 1, toks, HD), jnp.bfloat16))
        scratch.append(pltpu.VMEM((heads, ahead, toks, HD), jnp.bfloat16))
    scratch += [pltpu.SemaphoreType.DMA((5, parts)), pltpu.SemaphoreType.DMA((3 + parts,))]
    return pl.pallas_call(
        body,
        name=f"pack{first}",
        grid=(1,),
        in_specs=in_specs,
        out_specs=pl.BlockSpec(memory_space=pl.ANY),
        out_shape=jax.ShapeDtypeStruct((parts * heads, slots, toks, HD), jnp.bfloat16),
        scratch_shapes=scratch,
        compiler_params=params(),
    )(*args)


def nt(a, b):
    return lax.dot_general(a, b, (((1,), (1,)), ((), ())), preferred_element_type=jnp.float32)


def nn(a, b):
    return jnp.dot(a, b, preferred_element_type=jnp.float32)


def attend(pairs, message, source, first, per, count, groups, blocks, sums=None):
    devices, slots, toks, _ = message.shape
    srcs = devices // groups
    length = srcs * toks
    total = groups * blocks
    steps = groups * count
    last = sums is not None
    ahead = 0 if last else 2 * blocks
    behind = source.shape[1] - 1
    before = first // groups
    extra = 2 * blocks if last else 0

    def body(pair_ref, group_ref, m_ref, kv_ref, dots_ref, *refs):
        if last:
            sum_ref, out_ref = refs[:2]
            refs, (key_acc, value_acc) = refs[2:-2], refs[-2:]
        else:
            out_ref, sum_out = refs[:2]
            refs = refs[2:]
            key_acc, value_acc = sum_out.at[0], sum_out.at[1]
        keys, keys_t, values, dots = refs[:4]
        scores, prob_grads, probs, score_grads, queries, grads = (
            refs[4 + SLOTS * at : 4 + SLOTS * (at + 1)] for at in range(6)
        )
        for b in range(total):
            rows, at = slice(b // blocks * srcs, (b // blocks + 1) * srcs), b % blocks
            key = kv_ref[rows, at].reshape(length, HD)
            keys[b] = key
            keys_t[b] = key.astype(jnp.float32).T.astype(jnp.bfloat16)
            values[b] = kv_ref[rows, blocks + at].reshape(length, HD)
        row = lax.broadcasted_iota(jnp.int32, (PIECE, HD), 0)
        lane = lax.broadcasted_iota(jnp.int32, (PIECE, HD), 1)
        picks = jnp.where((lane % PIECE == row) & (lane < 3 * PIECE), 1.0, 0.0).astype(jnp.bfloat16)
        for g in range(groups):
            tile = dots_ref[g * srcs : (g + 1) * srcs, 0].reshape(length, HD)
            dots[g * PIECE : (g + 1) * PIECE] = nt(picks, tile)
        if last:
            key_acc[...] = sum_ref[0]
            value_acc[...] = sum_ref[1]
        else:
            sum_out[...] = jnp.zeros_like(sum_out)

        def where(c):
            group = lax.div(c, jnp.int32(count))
            return group, c - group * count

        def place(c, j):
            group, at = where(c)
            block = group * per + first + group_ref[0] * count + at
            return pair_ref[2 * block + j]

        def scores_of(c, slot):
            group, at = where(c)
            rows = pl.ds(group * srcs, srcs)
            query = m_ref[rows, ahead + at].reshape(length, HD)
            grad = m_ref[rows, ahead + count + at].reshape(length, HD)
            queries[slot][...] = query
            grads[slot][...] = grad
            for j in range(2):
                scores[slot][j] = nt(keys[place(c, j)], query)
                prob_grads[slot][j] = nt(values[place(c, j)], grad)

        def probs_of(c, slot):
            score, prob_grad = scores[slot], prob_grads[slot]
            cuts = [(j, slice(r, r + 32)) for j in range(2) for r in range(0, length, 32)]
            high = None
            for j, rows in cuts:
                part = jnp.max(score[j, rows].reshape(32 // 8, 8, length), axis=0)
                high = part if high is None else jnp.maximum(high, part)
            high = jnp.max(high, axis=0, keepdims=True) * EXP_SCALE
            norm = None
            for j, rows in cuts:
                weight = jnp.exp2(score[j, rows] * EXP_SCALE - high)
                score[j, rows] = weight
                part = jnp.sum(weight.reshape(32 // 8, 8, length), axis=0)
                norm = part if norm is None else norm + part
            inverse = 1.0 / jnp.sum(norm, axis=0, keepdims=True)
            group, at = where(c)
            dot_row = dots[pl.ds(group * PIECE + before + at, 1), :]
            for j, rows in cuts:
                prob = score[j, rows] * inverse
                probs[slot][j, rows] = prob.astype(jnp.bfloat16)
                score_grads[slot][j, rows] = (prob * (prob_grad[j, rows] - dot_row)).astype(
                    jnp.bfloat16
                )

        def grads_of(c, slot):
            value_part = nn(probs[slot][...].reshape(2 * length, length), grads[slot][...])
            key_part = nn(score_grads[slot][...].reshape(2 * length, length), queries[slot][...])
            query_t = None
            for j in range(2):
                b = place(c, j)
                rows = slice(j * length, (j + 1) * length)
                value_acc[b] += value_part[rows]
                key_acc[b] += key_part[rows]
                part = nn(keys_t[b], score_grads[slot][j])
                query_t = part if query_t is None else query_t + part
            group, at = where(c)
            rows = (query_t * SCALE).T.astype(jnp.bfloat16)
            out_ref[pl.ds(group * srcs, srcs), at] = rows.reshape(srcs, toks, HD)

        for ref in (probs[-1], score_grads[-1], queries[-1], grads[-1]):
            ref[...] = jnp.zeros_like(ref)
        scores_of(jnp.int32(0), 0)

        def several(i, _):
            for k in range(SLOTS):
                c = i * SLOTS + k
                grads_of(jnp.maximum(c - 1, 0), (k - 1) % SLOTS)
                scores_of(jnp.minimum(c + 1, steps - 1), (k + 1) % SLOTS)
                probs_of(c, k)
            return 0

        lax.fori_loop(0, steps // SLOTS, several, 0)
        grads_of(jnp.int32(steps - 1), SLOTS - 1)
        if last:
            for b in range(total):
                rows, at = slice(b // blocks * srcs, (b // blocks + 1) * srcs), count + b % blocks
                key_rows = (key_acc[b] * SCALE).astype(jnp.bfloat16)
                out_ref[rows, at] = key_rows.reshape(srcs, toks, HD)
                value_rows = value_acc[b].astype(jnp.bfloat16)
                out_ref[rows, at + blocks] = value_rows.reshape(srcs, toks, HD)

    def whole(shape):
        return pl.BlockSpec(shape, lambda i, p, g: (0,) * len(shape))

    dq = jax.ShapeDtypeStruct((devices, count + extra, toks, HD), jnp.bfloat16)
    acc = (2, total, length, HD)
    scratch = [
        pltpu.VMEM((total, length, HD), jnp.bfloat16),
        pltpu.VMEM((total, HD, length), jnp.bfloat16),
        pltpu.VMEM((total, length, HD), jnp.bfloat16),
        pltpu.VMEM((groups * PIECE, length), jnp.float32),
    ]
    scratch += [pltpu.VMEM((2, length, length), jnp.float32)] * (2 * SLOTS)
    scratch += [pltpu.VMEM((2, length, length), jnp.bfloat16)] * (2 * SLOTS)
    scratch += [pltpu.VMEM((length, HD), jnp.bfloat16)] * (2 * SLOTS)
    dots_spec = pl.BlockSpec((devices, 1, toks, HD), lambda i, p, g: (0, behind, 0, 0))
    in_specs = [whole(message.shape), whole((devices, 2 * blocks, toks, HD)), dots_spec]
    args = [message, source, source]
    if last:
        in_specs[0], args[0] = HELD, held(message)
        in_specs.append(whole(acc))
        args.append(sums)
        out_shape, out_specs = dq, whole(dq.shape)
        scratch += [pltpu.VMEM((total, length, HD), jnp.float32)] * 2
    else:
        out_shape = (dq, jax.ShapeDtypeStruct(acc, jnp.float32))
        out_specs = [whole(dq.shape), whole(acc)]
    flops = 2 * 5 * steps * length * 2 * length * HD
    return pl.pallas_call(
        body,
        name=f"attend{first}",
        grid_spec=pltpu.PrefetchScalarGridSpec(
            num_scalar_prefetch=2,
            grid=(1,),
            in_specs=in_specs,
            out_specs=out_specs,
            scratch_shapes=scratch,
        ),
        out_shape=out_shape,
        compiler_params=params(),
        cost_estimate=pl.CostEstimate(
            flops=flops, transcendentals=2 * steps * length * length, bytes_accessed=6 << 20
        ),
    )(*pairs, *args)


def unpack(message, total, first, count, step, groups, into=None, blocks=0):
    devices, _, toks, _ = message.shape
    heads = devices // groups
    width = heads * HD
    start = first // step
    per = count // step

    def body(m_ref, *refs):
        out_ref, *sums = refs if into is None else refs[1:]
        part = lax.div(pl.program_id(0), jnp.int32(per))
        at = (pl.program_id(0) - part * per) * step
        for h in range(heads):
            out_ref[:, :, h * HD : (h + 1) * HD] = m_ref[part * heads + h, pl.ds(at, step)]
        if blocks:

            @pl.when(pl.program_id(0) == 0)
            def _():
                for which, out in enumerate(sums):
                    behind = slice(count + which * blocks, count + (which + 1) * blocks)
                    for h in range(heads):
                        value = m_ref[h, behind].astype(jnp.float32)
                        for g in range(1, groups):
                            value += m_ref[g * heads + h, behind].astype(jnp.float32)
                        out[:, :, h * HD : (h + 1) * HD] = value.astype(jnp.bfloat16)

    in_specs = [HELD]
    args = [held(message)]
    out_shape = [jax.ShapeDtypeStruct((total, toks, width), message.dtype)]
    out_specs = [pl.BlockSpec((step, toks, width), lambda i: (start + i, 0, 0))]
    if blocks:
        out_shape += [jax.ShapeDtypeStruct((blocks, toks, width), message.dtype)] * 2
        out_specs += [pl.BlockSpec((blocks, toks, width), lambda i: (0, 0, 0))] * 2
    aliases = {}
    if into is not None:
        in_specs.append(pl.BlockSpec(memory_space=pl.ANY))
        args.append(into)
        aliases = {1: 0}
    return pl.pallas_call(
        body,
        name=f"unpack{first}",
        grid=(groups * per,),
        in_specs=in_specs,
        out_specs=out_specs,
        out_shape=out_shape,
        input_output_aliases=aliases,
        compiler_params=params(),
    )(*args)


def exchange(message):
    return lax.all_to_all(message, ("grp", "head"), split_axis=0, concat_axis=0, tiled=True)


def on_device(
    query, out_grad, forward_out, key_codes, key_scale, value_codes, value_scale, pairing
):
    per = query.shape[0]
    blocks = key_codes.shape[0]
    groups = lax.axis_size("grp")
    large = per * 2 // 3
    small = per - large
    pairs = pairing.reshape(-1)
    group = lax.axis_index("grp").reshape(1)
    codes = (key_codes, key_scale, value_codes, value_scale)
    got0 = exchange(pack(query, out_grad, 0, large, groups, forward_out, codes))
    later, pairs, group = lax.optimization_barrier((out_grad, pairs, group))
    got1 = exchange(pack(query, later, large, small, groups))
    pairs = (pairs, group)
    first, second = large // groups, small // groups
    grads0, sums = attend(pairs, got0, got0, 0, per, first, groups, blocks)
    back0 = exchange(grads0)
    grads1 = attend(pairs, got1, got0, large, per, second, groups, blocks, sums)
    back1 = exchange(grads1)
    (rows,) = unpack(back0, per, 0, first, 6, groups)
    return unpack(back1, per, large, second, 6, groups, into=rows, blocks=blocks)


def solution(mesh):
    spec = P("grp", "head", None)
    return jax.shard_map(
        on_device,
        mesh=mesh,
        in_specs=(spec,) * 7 + (P(),),
        out_specs=(spec,) * 3,
        check_vma=False,
    )
```
